512 devices in a mesh: row: 16 (over z_lo, core), col: 32 (over x, y, z_hi).
Axes of the slice: x: 4, y: 4, z: 16 (z_hi: 2, z_lo: 8; z = z_hi * 8 + z_lo), core: 2. Of those that a mesh axis runs over, the one named last changes fastest.
Arguments:
- features: bfloat16 [65536, 256], P(('row', 'col')), may hold values from -6 to 6
- blocks: bfloat16 [512, 128, 128, 128], P('row', 'col'), may hold values from -0.046875 to 0.046875
- block_col: int32 [512, 128], P('row', 'col'), may hold values from 0 to 15
- row_count: int32 [512, 32], P('row', 'col'), may hold values from 0 to 4, as said below
- weight: bfloat16 [256, 256], replicated, may hold values from -0.375 to 0.375
- out_bias: float32 [256], replicated, may hold values from -4 to 4
Outputs:
- layer_out: bfloat16 [65536, 256], P(('row', 'col'))
The draws below stay inside these ranges and needn't reach their ends.
Inputs may be any that keep to these rules, and one draw needn't show every extreme that they name: row_count[i, j] is how many of the 4 slots of block row i in column group j are in use; the others are ignored.
All inputs are finite; a program needn't handle non-finite values.
Results may differ from the reference program's by a relative error of at most 0.018.
Values may be sent and summed in bfloat16 or wider, within the bound.
No kernel may reach another device: no remote copies, remote signals or barrier semaphores. Data moves between devices by JAX's collectives and lax.ppermute only.
A program may use at most 64 MiB of HBM per device.

```python
import jax
import jax.numpy as jnp
from jax import lax

F = 256
BS = 128
KR = 4
RB = 32
CB = 16
BROWS = 512
NODES = 65536
N_ROW = 16
N_COL = 32


def draw_row_count(key, part):
    subkeys = jax.random.split(key, 5)
    base_count = jax.random.randint(subkeys[0], (BROWS, N_COL), 0, KR // 2 + 1)
    full_rows = jax.random.randint(subkeys[1], (BROWS, N_COL), 0, 8) == 0
    heavy_dev = jax.random.randint(subkeys[2], (N_ROW, N_COL), 0, 4) == 0
    heavy_rows = jnp.repeat(heavy_dev, RB, axis=0)
    counts = jnp.where(full_rows | heavy_rows, KR, base_count)
    pick_row = jax.random.randint(subkeys[3], (), 0, BROWS)
    pick_col = jax.random.randint(subkeys[4], (), 0, N_COL)
    return counts.at[pick_row, pick_col].set(KR).astype(jnp.int32)


def with_ends(values, own_key, low, top_value):
    longest = values.shape.index(max(values.shape))
    spots = []
    for shift in (0, 1):
        where = [jax.random.randint(jax.random.fold_in(own_key, axis), (), 0, length) for axis, length in enumerate(values.shape)]
        where[longest] = (where[longest] + shift) % values.shape[longest]
        spots.append(tuple(where))
    return values.at[spots[0]].set(low).at[spots[1]].set(top_value)


def level_of(own_key, shape, pieces, low, top_value):
    gain, own = 1.0, jax.random.fold_in(own_key, 6)
    for position, shards_of in pieces:
        steps = jnp.exp(jax.random.uniform(jax.random.fold_in(own, position), (shards_of,), jnp.float32, low / len(pieces), top_value / len(pieces)))
        gain = gain * jnp.repeat(steps, shape[position] // shards_of).reshape([-1 if axis == position else 1 for axis in range(len(shape))])
    return gain


def gaussian(key, dims, deviation, most, cuts=(), kind=jnp.bfloat16):
    level = level_of(key, dims, cuts, -0.22, 0.18) if cuts else 1.0
    values = jax.random.normal(key, dims, jnp.float32) * deviation * level
    return jnp.minimum(jnp.maximum(values, -most), most).astype(kind)


def setup_inputs(seed: int = 0) -> dict:
    arg_keys = jax.random.split(jax.random.key(seed), 7)
    features = gaussian(arg_keys[0], (NODES, F), 1.0, 6.0, ((0, 512),))
    blocks = gaussian(arg_keys[1], (BROWS, N_COL * KR, BS, BS), (BS * KR * N_COL) ** -0.5, 0.046875, ((0, 16), (1, 32)))
    block_col = with_ends(jax.random.randint(arg_keys[2], (BROWS, N_COL * KR), 0, CB), jax.random.fold_in(arg_keys[2], 1), 0, CB - 1).astype(jnp.int32)
    row_count = draw_row_count(jax.random.fold_in(arg_keys[6], 71), 0)
    weight = gaussian(arg_keys[4], (F, F), F ** -0.5, 0.375)
    out_bias = gaussian(arg_keys[5], (F,), 1.0, 4.0, (), jnp.float32)
    return dict(features=features, blocks=blocks, block_col=block_col, row_count=row_count, weight=weight, out_bias=out_bias)


def local_terms(blocks, block_col, counts, stripe):
    slot_ids = jnp.arange(block_col.shape[1], dtype=jnp.int32)[None, :]
    live_slots = (slot_ids < counts).astype(jnp.float32)
    picked = stripe[block_col].astype(jnp.float32) * live_slots[:, :, None, None]
    term_rows = jnp.einsum("ikab,ikbf->iaf", blocks.astype(jnp.float32), picked, precision=lax.Precision.HIGHEST)
    return term_rows.reshape(-1, stripe.shape[2])


def reference(features, blocks, block_col, row_count, weight, out_bias):
    feat_width = features.shape[1]
    block_size = blocks.shape[2]
    per_device = features.shape[0] // (N_ROW * N_COL)
    band_rows = blocks.shape[0] // N_ROW
    slot_count = blocks.shape[1] // N_COL
    grid_feat = features.reshape(N_ROW, N_COL, per_device, feat_width)
    stripes = jnp.transpose(grid_feat, (1, 0, 2, 3)).reshape(N_COL, -1, block_size, feat_width)
    grid_blocks = blocks.reshape(N_ROW, band_rows, N_COL, slot_count, block_size, block_size)
    grid_cols = block_col.reshape(N_ROW, band_rows, N_COL, slot_count)
    grid_counts = row_count.reshape(N_ROW, band_rows, N_COL)

    def one_band(packed):
        band_blocks, band_cols, band_counts = packed
        moved_blocks = jnp.moveaxis(band_blocks, 1, 0)
        moved_cols = jnp.moveaxis(band_cols, 1, 0)
        moved_counts = jnp.moveaxis(band_counts, 1, 0)

        def add_group(total, items):
            grp_blocks, grp_cols, grp_counts, grp_stripe = items
            term_rows = local_terms(grp_blocks, grp_cols, grp_counts[:, None], grp_stripe)
            rounded = lax.optimization_barrier(term_rows.astype(jnp.bfloat16))
            return total + rounded.astype(jnp.float32), None

        start_total = jnp.zeros((band_rows * block_size, feat_width), jnp.float32)
        total, _ = lax.scan(add_group, start_total, (moved_blocks, moved_cols, moved_counts, stripes))
        return total

    aggregate = lax.map(one_band, (grid_blocks, grid_cols, grid_counts)).reshape(-1, feat_width)
    hidden = jnp.dot(aggregate.astype(jnp.bfloat16), weight, preferred_element_type=jnp.float32) + out_bias
    return jnp.maximum(hidden, 0.0).astype(jnp.bfloat16)
```

```python
import jax
import jax.numpy as jnp
from jax import lax
from jax.experimental import pallas as pl
from jax.experimental.pallas import tpu as pltpu
from jax.sharding import Mesh, PartitionSpec as P

ZL, CORE, X, Y, ZH = 8, 2, 4, 4, 2
SLOTS, BS, F = 4, 128, 256


def swap(value, axis, size, bit):
    return lax.ppermute(value, axis, [(i, i ^ bit) for i in range(size)])


def terms_kernel(me_ref, cols_ref, counts_ref, blocks_ref, stripe_ref, out_ref):
    rows = blocks_ref.shape[0]
    base = pl.program_id(0) * rows
    me = me_ref[0]
    for i in range(rows):
        count = counts_ref[base + i]
        lhs, rhs = [], []
        for k in range(SLOTS):
            offset = cols_ref[(base + i) * SLOTS + k] ^ me
            spot = (
                ((offset & 1) << 3)
                | ((offset & 2) << 1)
                | ((offset & 4) >> 1)
                | ((offset & 8) >> 3)
            )
            block = blocks_ref[i, k]
            lhs.append(jnp.where(k < count, block, jnp.zeros_like(block)))
            rhs.append(stripe_ref[spot])
        term = jnp.dot(
            jnp.concatenate(lhs, axis=1),
            jnp.concatenate(rhs, axis=0),
            preferred_element_type=jnp.float32,
        )
        out_ref[i] = term.astype(jnp.bfloat16)


def terms(me, cols, counts, blocks, stripe):
    rows = blocks.shape[0]
    step = 8
    return pl.pallas_call(
        terms_kernel,
        grid_spec=pltpu.PrefetchScalarGridSpec(
            num_scalar_prefetch=3,
            grid=(rows // step,),
            in_specs=[
                pl.BlockSpec((step, SLOTS, BS, BS), lambda i, *_: (i, 0, 0, 0)),
                pl.BlockSpec((16, BS, F), lambda i, *_: (0, 0, 0)),
            ],
            out_specs=pl.BlockSpec((step, BS, F), lambda i, *_: (i, 0, 0)),
        ),
        out_shape=jax.ShapeDtypeStruct((rows, BS, F), jnp.bfloat16),
        compiler_params=pltpu.CompilerParams(vmem_limit_bytes=12 << 20),
        cost_estimate=pl.CostEstimate(
            flops=2 * rows * SLOTS * BS * BS * F, bytes_accessed=8 << 20, transcendentals=0
        ),
        name="terms",
    )(me, cols, counts, blocks, stripe)


def sum_kernel(zh_ref, parts_ref, own_ref, send_ref):
    zh = zh_ref[0]

    def total(which):
        acc = parts_ref[0, which].astype(jnp.float32)
        for i in range(1, parts_ref.shape[0]):
            acc = acc + parts_ref[i, which].astype(jnp.float32)
        return acc

    own_ref[...] = total(zh)
    send_ref[...] = total(1 - zh).astype(jnp.bfloat16)


def partial_sums(zh, parts):
    return pl.pallas_call(
        sum_kernel,
        in_specs=[
            pl.BlockSpec(memory_space=pltpu.SMEM),
            pl.BlockSpec(memory_space=pltpu.VMEM),
        ],
        out_specs=[pl.BlockSpec(memory_space=pltpu.VMEM)] * 2,
        out_shape=[
            jax.ShapeDtypeStruct((BS, F), jnp.float32),
            jax.ShapeDtypeStruct((BS, F), jnp.bfloat16),
        ],
        compiler_params=pltpu.CompilerParams(vmem_limit_bytes=8 << 20),
        name="partial_sums",
    )(zh, parts)


def finish_kernel(own_ref, other_ref, weight_ref, bias_ref, out_ref):
    summed = own_ref[...] + other_ref[...].astype(jnp.float32)
    hidden = jnp.dot(
        summed.astype(jnp.bfloat16),
        weight_ref[...],
        preferred_element_type=jnp.float32,
    )
    out_ref[...] = jnp.maximum(hidden + bias_ref[...], 0.0).astype(jnp.bfloat16)


def finish(own, other, weight, bias):
    return pl.pallas_call(
        finish_kernel,
        in_specs=[pl.BlockSpec(memory_space=pltpu.VMEM)] * 4,
        out_specs=pl.BlockSpec(memory_space=pltpu.VMEM),
        out_shape=jax.ShapeDtypeStruct((BS, F), jnp.bfloat16),
        compiler_params=pltpu.CompilerParams(vmem_limit_bytes=4 << 20),
        name="finish",
    )(own, other, weight, bias)


def local(features, blocks, block_col, row_count, weight, out_bias):
    me = (lax.axis_index("zl") * CORE + lax.axis_index("core")).astype(jnp.int32)
    zh = lax.axis_index("zh").astype(jnp.int32)
    held = features[None]
    for axis, size, bit in (("zl", ZL, 4), ("zl", ZL, 2), ("zl", ZL, 1), ("core", CORE, 1)):
        held = jnp.concatenate([held, swap(held, axis, size, bit)], axis=0)
    value = terms(
        me[None], block_col.reshape(-1), row_count.reshape(-1), blocks, held
    )
    parts = lax.all_to_all(
        value.reshape(X * Y, ZH, BS, F), ("x", "y"), 0, 0
    )
    own, send = partial_sums(zh[None], parts)
    other = swap(send, "zh", ZH, 1)
    return finish(own, other, weight, out_bias[None])


def solution(mesh):
    fine = Mesh(
        mesh.devices.reshape(ZL, CORE, X, Y, ZH), ("zl", "core", "x", "y", "zh")
    )
    row, col = ("zl", "core"), ("x", "y", "zh")
    return jax.shard_map(
        local,
        mesh=fine,
        in_specs=(
            P(row + col, None),
            P(row, col, None, None),
            P(row, col),
            P(row, col),
            P(),
            P(),
        ),
        out_specs=P(row + col, None),
        check_vma=False,
    )
```

```python
import jax
import jax.numpy as jnp
from jax import lax
from jax.experimental import pallas as pl
from jax.experimental.pallas import tpu as pltpu
from jax.sharding import Mesh, PartitionSpec as P

ZL, CORE, X, Y, ZH = 8, 2, 4, 4, 2
SLOTS, BS, F = 4, 128, 256
VMEM = pl.BlockSpec(memory_space=pltpu.VMEM)
SMEM = pl.BlockSpec(memory_space=pltpu.SMEM)


def swap(value, axis, size, bit):
    return lax.ppermute(value, axis, [(i, i ^ bit) for i in range(size)])


def whole(kernel, ins, out_shape, name, cost, limit=4 << 20):
    return pl.pallas_call(
        kernel,
        in_specs=[SMEM if a.dtype == jnp.int32 else VMEM for a in ins],
        out_specs=jax.tree.map(lambda _: VMEM, out_shape),
        out_shape=out_shape,
        compiler_params=pltpu.CompilerParams(vmem_limit_bytes=limit),
        cost_estimate=pl.CostEstimate(
            flops=cost[0], bytes_accessed=cost[1], transcendentals=0
        ),
        name=name,
    )(*ins)


def side_by_side(counts_ref, row, block_of):
    count = counts_ref[0, row]
    lhs = []
    for k in range(SLOTS):
        block = block_of(k)
        lhs.append(jnp.where(k < count, block, jnp.zeros_like(block)))
    return jnp.concatenate(lhs, axis=1)


def product(place_ref, cols_ref, row, lhs, stripe_ref):
    rhs = [stripe_ref[cols_ref[k, row] ^ place_ref[0]] for k in range(SLOTS)]
    term = jnp.dot(
        lhs, jnp.concatenate(rhs, axis=0), preferred_element_type=jnp.float32
    )
    return term.astype(jnp.bfloat16)


def lhs_kernel(place_ref, counts_ref, blocks_ref, out_ref):
    step = blocks_ref.shape[0]
    base = pl.program_id(0) * step
    half = 1 - place_ref[1]
    for i in range(step):
        out_ref[i] = side_by_side(
            counts_ref, 2 * (base + i) + half, lambda k: blocks_ref[i, 0, k]
        )


def near_kernel(place_ref, counts_ref, cols_ref, blocks_ref, stripe_ref, out_ref):
    step = blocks_ref.shape[0]
    base = pl.program_id(0) * step
    for i in range(step):
        row = 2 * (base + i) + place_ref[1]
        lhs = side_by_side(counts_ref, row, lambda k: blocks_ref[i, 0, k])
        out_ref[i] = product(place_ref, cols_ref, row, lhs, stripe_ref)


def on_blocks(kernel, scalars, blocks, more, width, far, name, cost):
    step = 4

    def pick(i, place_ref, *_):
        return (i, 1 - place_ref[1] if far else place_ref[1], 0, 0, 0)

    return pl.pallas_call(
        kernel,
        grid_spec=pltpu.PrefetchScalarGridSpec(
            num_scalar_prefetch=len(scalars),
            grid=(X * Y // step,),
            in_specs=[pl.BlockSpec((step, 1, SLOTS, BS, BS), pick)]
            + [VMEM for _ in more],
            out_specs=pl.BlockSpec((step, BS, width), lambda i, *_: (i, 0, 0)),
        ),
        out_shape=jax.ShapeDtypeStruct((X * Y, BS, width), jnp.bfloat16),
        compiler_params=pltpu.CompilerParams(vmem_limit_bytes=8 << 20),
        cost_estimate=pl.CostEstimate(
            flops=cost[0], bytes_accessed=cost[1], transcendentals=0
        ),
        name=name,
    )(*scalars, pltpu.with_memory_space_constraint(blocks, pltpu.HBM), *more)


def far_kernel(place_ref, cols_ref, lhs_ref, *refs):
    p0, p1, p2, p4, p53, p6, p7, far0, far1, stripe_ref, out_ref = refs
    near = (p0, p1, p2, p53.at[1], p4, p53.at[0], p6, p7)
    across = [far0.at[i] for i in range(4)] + [far1.at[i] for i in range(4)]
    for offset in range(ZL):
        stripe_ref[2 * offset] = near[offset][...]
        stripe_ref[2 * offset + 1] = across[(0, 1, 2, 4, 5, 3, 6, 7).index(offset)][...]
    for j in range(out_ref.shape[0]):
        row = 2 * j + 1 - place_ref[1]
        out_ref[j] = product(place_ref, cols_ref, row, lhs_ref[j], stripe_ref)


def total(parts_ref):
    acc = parts_ref[0].astype(jnp.float32)
    for i in range(1, parts_ref.shape[0]):
        acc = acc + parts_ref[i].astype(jnp.float32)
    return acc


def send_kernel(parts_ref, out_ref):
    out_ref[...] = total(parts_ref).astype(jnp.bfloat16)


def finish_kernel(parts_ref, other_ref, weight_ref, bias_ref, out_ref):
    summed = total(parts_ref) + other_ref[...].astype(jnp.float32)
    hidden = jnp.dot(
        summed.astype(jnp.bfloat16),
        weight_ref[...],
        preferred_element_type=jnp.float32,
    )
    out_ref[...] = jnp.maximum(hidden + bias_ref[...], 0.0).astype(jnp.bfloat16)


def local(features, blocks, block_col, row_count, weight, out_bias):
    bf16 = jnp.bfloat16
    place = jnp.stack(
        [lax.axis_index("zl") * CORE + lax.axis_index("core"), lax.axis_index("zh")]
    ).astype(jnp.int32)
    cols, counts = block_col.T, row_count.T
    blocks = blocks.reshape(X * Y, ZH, SLOTS, BS, BS)
    far_lhs = on_blocks(
        lhs_kernel, [place, counts], blocks, [], SLOTS * BS, True, "far_lhs", (0, 4 << 20)
    )
    p = {0: features}
    p[4] = swap(p[0], "zl", ZL, 4)
    p[2] = swap(p[0], "zl", ZL, 2)
    p[1] = swap(p[0], "zl", ZL, 1)
    p[6] = swap(p[4], "zl", ZL, 2)
    p53 = swap(jnp.stack([p[4], p[2]]), "zl", ZL, 1)
    p[6], far_lhs = lax.optimization_barrier((p[6], far_lhs))
    p[7] = swap(p[6], "zl", ZL, 1)
    far0 = swap(jnp.stack([p[0], p[1], p[2], p[4]]), "core", CORE, 1)
    far1 = swap(
        jnp.concatenate([p53, p[6][None], p[7][None]], axis=0), "core", CORE, 1
    )
    half = jax.ShapeDtypeStruct((X * Y, BS, F), bf16)
    work = (2 * X * Y * SLOTS * BS * BS * F, 4 << 20)
    stripe, far_terms = whole(
        far_kernel,
        [place, cols, far_lhs, p[0], p[1], p[2], p[4], p53, p[6], p[7], far0, far1],
        [half, half],
        "far_terms",
        work,
    )
    near_terms = on_blocks(
        near_kernel, [place, counts, cols], blocks, [stripe], F, False, "near_terms", work
    )
    far_parts = lax.all_to_all(far_terms, ("x", "y"), 0, 0)
    near_parts = lax.all_to_all(near_terms, ("x", "y"), 0, 0)
    out = jax.ShapeDtypeStruct((BS, F), bf16)
    send = whole(send_kernel, [far_parts], out, "send", (0, 1 << 20))
    other = swap(send, "zh", ZH, 1)
    return whole(
        finish_kernel,
        [near_parts, other, weight, out_bias[None]],
        out,
        "finish",
        (2 * BS * F * F, 2 << 20),
    )


def solution(mesh):
    fine = Mesh(
        mesh.devices.reshape(ZL, CORE, X, Y, ZH), ("zl", "core", "x", "y", "zh")
    )
    row, col = ("zl", "core"), ("x", "y", "zh")
    return jax.shard_map(
        local,
        mesh=fine,
        in_specs=(
            P(row + col, None),
            P(row, col, None, None),
            P(row, col),
            P(row, col),
            P(),
            P(),
        ),
        out_specs=P(row + col, None),
        check_vma=False,
    )
```

```python
import jax
import jax.numpy as jnp
from jax import lax
from jax.experimental import pallas as pl
from jax.experimental.pallas import tpu as pltpu
from jax.sharding import Mesh, PartitionSpec as P

ZL, CORE, X, Y, ZH = 8, 2, 4, 4, 2
SLOTS, BS, F = 4, 128, 256
VMEM = pl.BlockSpec(memory_space=pltpu.VMEM)
SMEM = pl.BlockSpec(memory_space=pltpu.SMEM)


def swap(value, axis, size, bit):
    return lax.ppermute(value, axis, [(i, i ^ bit) for i in range(size)])


def whole(kernel, ins, out_shape, name, cost, limit=4 << 20):
    return pl.pallas_call(
        kernel,
        in_specs=[SMEM if a.dtype == jnp.int32 else VMEM for a in ins],
        out_specs=jax.tree.map(lambda _: VMEM, out_shape),
        out_shape=out_shape,
        compiler_params=pltpu.CompilerParams(vmem_limit_bytes=limit),
        cost_estimate=pl.CostEstimate(
            flops=cost[0], bytes_accessed=cost[1], transcendentals=0
        ),
        name=name,
    )(*ins)


def side_by_side(table_ref, row, block_of):
    count = table_ref[SLOTS, row]
    lhs = []
    for k in range(SLOTS):
        block = block_of(k)
        lhs.append(jnp.where(k < count, block, jnp.zeros_like(block)))
    return jnp.concatenate(lhs, axis=1)


def product(table_ref, row, lhs, stripe_ref):
    rhs = [stripe_ref[table_ref[k, row]] for k in range(SLOTS)]
    term = jnp.dot(
        lhs, jnp.concatenate(rhs, axis=0), preferred_element_type=jnp.float32
    )
    return term.astype(jnp.bfloat16)


def near_kernel(table_ref, blocks_ref, stripe_ref, out_ref):
    step = blocks_ref.shape[0]
    base = pl.program_id(0) * step
    for i in range(step):
        row = 2 * (base + i) + table_ref[SLOTS + 1, 0]
        lhs = side_by_side(table_ref, row, lambda k: blocks_ref[i, 0, k])
        out_ref[i] = product(table_ref, row, lhs, stripe_ref)


def near_half(table, blocks, stripe, cost):
    step = 4

    def pick(i, table_ref):
        return (i, table_ref[SLOTS + 1, 0], 0, 0, 0)

    return pl.pallas_call(
        near_kernel,
        grid_spec=pltpu.PrefetchScalarGridSpec(
            num_scalar_prefetch=1,
            grid=(X * Y // step,),
            in_specs=[pl.BlockSpec((step, 1, SLOTS, BS, BS), pick), VMEM],
            out_specs=pl.BlockSpec((step, BS, F), lambda i, *_: (i, 0, 0)),
        ),
        out_shape=jax.ShapeDtypeStruct((X * Y, BS, F), jnp.bfloat16),
        compiler_params=pltpu.CompilerParams(vmem_limit_bytes=8 << 20),
        cost_estimate=pl.CostEstimate(
            flops=cost[0], bytes_accessed=cost[1], transcendentals=0
        ),
        name="near_terms",
    )(table, pltpu.with_memory_space_constraint(blocks, pltpu.HBM), stripe)


def far_kernel(table_ref, blocks_ref, *refs):
    trio, p6, ones, p7, core0, core1 = refs[:6]
    stripe_ref, out_ref, held, made, in_sem, out_sem = refs[6:]
    half = 1 - table_ref[SLOTS + 1, 0]
    rows = X * Y
    loads = [
        pltpu.make_async_copy(blocks_ref.at[j, half], held.at[j], in_sem.at[j])
        for j in range(rows)
    ]
    stores = [
        pltpu.make_async_copy(made.at[j], out_ref.at[j], out_sem.at[j])
        for j in range(rows)
    ]
    for load in loads:
        load.start()
    near = (
        trio.at[0],
        ones.at[0],
        trio.at[2],
        ones.at[2],
        trio.at[1],
        ones.at[1],
        p6,
        p7,
    )
    across = [core0.at[i] for i in range(4)] + [core1.at[i] for i in range(4)]
    order = (0, 4, 2, 6, 1, 5, 3, 7)
    for offset in range(ZL):
        stripe_ref[2 * offset] = near[offset][...]
        stripe_ref[2 * offset + 1] = across[order.index(offset)][...]
    for j in range(rows):
        row = 2 * j + half
        loads[j].wait()
        lhs = side_by_side(table_ref, row, lambda k: held[j, k])
        made[j] = product(table_ref, row, lhs, stripe_ref)
        stores[j].start()
    for store in stores:
        store.wait()


def far_half(table, blocks, pieces, cost):
    half = (X * Y, BS, F)
    return pl.pallas_call(
        far_kernel,
        in_specs=[SMEM, pl.BlockSpec(memory_space=pl.ANY)] + [VMEM] * len(pieces),
        out_specs=[VMEM, pl.BlockSpec(memory_space=pl.ANY)],
        out_shape=[jax.ShapeDtypeStruct(half, jnp.bfloat16)] * 2,
        scratch_shapes=[
            pltpu.VMEM((X * Y, SLOTS, BS, BS), jnp.bfloat16),
            pltpu.VMEM(half, jnp.bfloat16),
            pltpu.SemaphoreType.DMA((X * Y,)),
            pltpu.SemaphoreType.DMA((X * Y,)),
        ],
        compiler_params=pltpu.CompilerParams(vmem_limit_bytes=10 << 20),
        cost_estimate=pl.CostEstimate(
            flops=cost[0], bytes_accessed=cost[1], transcendentals=0
        ),
        name="far_terms",
    )(table, pltpu.with_memory_space_constraint(blocks, pltpu.HBM), *pieces)


def total(parts_ref):
    acc = parts_ref[0].astype(jnp.float32)
    for i in range(1, parts_ref.shape[0]):
        acc = acc + parts_ref[i].astype(jnp.float32)
    return acc


def send_kernel(parts_ref, out_ref):
    out_ref[...] = total(parts_ref).astype(jnp.bfloat16)


def finish_kernel(parts_ref, other_ref, weight_ref, bias_ref, out_ref):
    summed = total(parts_ref) + other_ref[...].astype(jnp.float32)
    hidden = jnp.dot(
        summed.astype(jnp.bfloat16),
        weight_ref[...],
        preferred_element_type=jnp.float32,
    )
    out_ref[...] = jnp.maximum(hidden + bias_ref[...], 0.0).astype(jnp.bfloat16)


def local(features, blocks, block_col, row_count, weight, out_bias):
    bf16 = jnp.bfloat16
    me = (lax.axis_index("zl") * CORE + lax.axis_index("core")).astype(jnp.int32)
    zh = lax.axis_index("zh").astype(jnp.int32)
    table = jnp.concatenate(
        [block_col.T ^ me, row_count.T, jnp.full_like(row_count.T, zh)], axis=0
    )
    blocks = blocks.reshape(X * Y, ZH, SLOTS, BS, BS)
    p = {0: features}
    p[4] = swap(p[0], "zl", ZL, 4)
    p[2] = swap(p[0], "zl", ZL, 2)
    p[4], table = lax.optimization_barrier((p[4], table))
    p[6] = swap(p[4], "zl", ZL, 2)
    trio = jnp.stack([p[0], p[4], p[2]])
    ones = swap(trio, "zl", ZL, 1)
    p[7] = swap(p[6], "zl", ZL, 1)
    core0 = swap(jnp.concatenate([trio, p[6][None]], axis=0), "core", CORE, 1)
    core1 = swap(jnp.concatenate([ones, p[7][None]], axis=0), "core", CORE, 1)
    work = (2 * X * Y * SLOTS * BS * BS * F, 4 << 20)
    stripe, far_terms = far_half(
        table,
        blocks,
        [trio, p[6], ones, p[7], core0, core1],
        work,
    )
    near_terms = near_half(table, blocks, stripe, work)
    far_parts = lax.all_to_all(far_terms, ("x", "y"), 0, 0)
    near_parts = lax.all_to_all(near_terms, ("x", "y"), 0, 0)
    out = jax.ShapeDtypeStruct((BS, F), bf16)
    send = whole(send_kernel, [far_parts], out, "send", (0, 1 << 20))
    other = swap(send, "zh", ZH, 1)
    return whole(
        finish_kernel,
        [near_parts, other, weight, out_bias[None]],
        out,
        "finish",
        (2 * BS * F * F, 2 << 20),
    )


def solution(mesh):
    fine = Mesh(
        mesh.devices.reshape(ZL, CORE, X, Y, ZH), ("zl", "core", "x", "y", "zh")
    )
    row, col = ("zl", "core"), ("x", "y", "zh")
    return jax.shard_map(
        local,
        mesh=fine,
        in_specs=(
            P(row + col, None),
            P(row, col, None, None),
            P(row, col),
            P(row, col),
            P(),
            P(),
        ),
        out_specs=P(row + col, None),
        check_vma=False,
    )
```

```python
import jax
import jax.numpy as jnp
from jax import lax
from jax.experimental import pallas as pl
from jax.experimental.pallas import tpu as pltpu
from jax.sharding import Mesh, PartitionSpec as P

ZL, CORE, X, Y, ZH = 8, 2, 4, 4, 2
SLOTS, BS, F = 4, 128, 256
COUNT, HALF, SIDE = SLOTS, SLOTS + 1, SLOTS + 2
VMEM = pl.BlockSpec(memory_space=pltpu.VMEM)
SMEM = pl.BlockSpec(memory_space=pltpu.SMEM)
ANY = pl.BlockSpec(memory_space=pl.ANY)
STEPS = ((4, 2, 1), (2, 4, 1))


def whole(kernel, ins, out_shape, name, cost, limit=4 << 20, specs=None, scratch=()):
    return pl.pallas_call(
        kernel,
        in_specs=specs or [VMEM] * len(ins),
        out_specs=jax.tree.map(lambda _: VMEM, out_shape),
        out_shape=out_shape,
        scratch_shapes=scratch,
        compiler_params=pltpu.CompilerParams(vmem_limit_bytes=limit),
        cost_estimate=pl.CostEstimate(
            flops=cost[0], bytes_accessed=cost[1], transcendentals=0
        ),
        name=name,
    )(*ins)


def copy_kernel(in_ref, out_ref):
    out_ref[...] = in_ref[...]


def side_by_side(table_ref, row, block_of):
    count = table_ref[COUNT, row]
    lhs = []
    for k in range(SLOTS):
        block = block_of(k)
        lhs.append(jnp.where(k < count, block, jnp.zeros_like(block)))
    return jnp.concatenate(lhs, axis=1)


def product(table_ref, row, lhs, stripe_ref):
    rhs = [stripe_ref[table_ref[k, row]] for k in range(SLOTS)]
    term = jnp.dot(
        lhs, jnp.concatenate(rhs, axis=0), preferred_element_type=jnp.float32
    )
    return term.astype(jnp.bfloat16)


def far_lhs_kernel(table_ref, blocks_ref, out_ref):
    step = blocks_ref.shape[0]
    base = pl.program_id(0) * step
    for i in range(step):
        row = 2 * (base + i) + 1 - table_ref[HALF, 0]
        out_ref[i] = side_by_side(table_ref, row, lambda k: blocks_ref[i, 0, k])


def far_lhs_rows(table, blocks):
    step = 4
    return pl.pallas_call(
        far_lhs_kernel,
        grid_spec=pltpu.PrefetchScalarGridSpec(
            num_scalar_prefetch=1,
            grid=(X * Y // step,),
            in_specs=[
                pl.BlockSpec(
                    (step, 1, SLOTS, BS, BS),
                    lambda i, table_ref: (i, 1 - table_ref[HALF, 0], 0, 0, 0),
                )
            ],
            out_specs=pl.BlockSpec((step, BS, SLOTS * BS), lambda i, *_: (i, 0, 0)),
        ),
        out_shape=jax.ShapeDtypeStruct((X * Y, BS, SLOTS * BS), jnp.bfloat16),
        compiler_params=pltpu.CompilerParams(vmem_limit_bytes=6 << 20),
        cost_estimate=pl.CostEstimate(
            flops=0, bytes_accessed=4 << 20, transcendentals=0
        ),
        name="far_lhs",
    )(table, blocks)


def terms_kernel(
    table_ref, blocks_ref, lhs_ref, near_ref, across_ref, out_ref, stripe_ref, held, sem
):
    zh, side = table_ref[HALF, 0], table_ref[SIDE, 0]
    rows = X * Y
    loads = [
        pltpu.make_async_copy(blocks_ref.at[j, zh], held.at[j], sem.at[j])
        for j in range(rows)
    ]
    for load in loads:
        load.start()
    stripe_ref[:ZL] = near_ref[...]
    stripe_ref[ZL:] = across_ref[...]

    def spot(k, m):
        return jnp.where(side == 0, k * Y + m, m * Y + k)

    for k in range(X):
        for m in range(Y):
            j = spot(k, m)
            out_ref[k, 0, m] = product(
                table_ref, 2 * j + 1 - zh, lhs_ref[j], stripe_ref
            )
    for load in loads:
        load.wait()
    for k in range(X):
        for m in range(Y):
            j = spot(k, m)
            row = 2 * j + zh
            lhs = side_by_side(table_ref, row, lambda s: held[j, s])
            out_ref[k, 1, m] = product(table_ref, row, lhs, stripe_ref)


def total(parts):
    acc = parts[0].astype(jnp.float32)
    for part in parts[1:]:
        acc = acc + part.astype(jnp.float32)
    return acc


def stage_kernel(parts_ref, out_ref):
    for half in range(2):
        for m in range(Y):
            out_ref[m, half] = total(
                [parts_ref[k, half, m] for k in range(X)]
            ).astype(jnp.bfloat16)


def send_kernel(parts_ref, out_ref):
    out_ref[...] = total([parts_ref[k, 0] for k in range(Y)]).astype(jnp.bfloat16)


def finish_kernel(parts_ref, other_ref, weight_ref, bias_ref, out_ref):
    summed = total([parts_ref[k, 1] for k in range(Y)]) + other_ref[...].astype(
        jnp.float32
    )
    hidden = jnp.dot(
        summed.astype(jnp.bfloat16),
        weight_ref[...],
        preferred_element_type=jnp.float32,
    )
    out_ref[...] = jnp.maximum(hidden + bias_ref[...], 0.0).astype(jnp.bfloat16)


def along(first):
    by_x = [[x * Y + y for x in range(X)] for y in range(Y)]
    by_y = [[x * Y + y for y in range(Y)] for x in range(X)]
    sides = (by_x, by_y) if first else (by_y, by_x)
    return [[c * X * Y + i for i in g] for c, gs in enumerate(sides) for g in gs]


def exchange(value, first):
    return lax.all_to_all(
        value, ("core", "x", "y"), 0, 0, axis_index_groups=along(first)
    )


def shard_table(block_col, row_count):
    zl, core, zh = (
        lax.axis_index(a).astype(jnp.int32) for a in ("zl", "core", "zh")
    )
    col = block_col.T
    offset, side = (col >> 1) ^ zl, col & 1
    high, mid = (offset >> 2) & 1, (offset >> 1) & 1
    first = jnp.where(side == 0, high, mid)
    second = jnp.where(side == 0, mid, high)
    spots = first + 2 * second + 4 * (offset & 1) + 8 * (side ^ core)
    counts = row_count.T
    return jnp.concatenate(
        [spots, counts, jnp.full_like(counts, zh), jnp.full_like(counts, core)], axis=0
    )


def local(features, blocks, block_col, row_count, weight, out_bias):
    bf16 = jnp.bfloat16
    table = shard_table(block_col, row_count)
    blocks = pltpu.with_memory_space_constraint(
        blocks.reshape(X * Y, ZH, SLOTS, BS, BS), pltpu.HBM
    )
    own = whole(
        copy_kernel,
        [features[None]],
        jax.ShapeDtypeStruct((1, BS, F), bf16),
        "own",
        (0, 1 << 17),
    )
    held = own
    for step in range(3):
        came = lax.ppermute(
            features[None] if step == 0 else held,
            ("zl", "core"),
            [
                (z * CORE + c, (z ^ STEPS[c][step]) * CORE + c)
                for z in range(ZL)
                for c in range(CORE)
            ],
        )
        if step == 0:
            came, table = lax.optimization_barrier((came, table))
            far_lhs = far_lhs_rows(table, blocks)
        if step == 1:
            came, far_lhs = lax.optimization_barrier((came, far_lhs))
        held = jnp.concatenate([held, came], axis=0)
    across = lax.ppermute(held, "core", [(0, 1), (1, 0)])
    shape = (X, 2, Y, BS, F)
    terms = whole(
        terms_kernel,
        [table, blocks, far_lhs, held, across],
        jax.ShapeDtypeStruct(shape, bf16),
        "terms",
        (2 * X * Y * 2 * SLOTS * BS * BS * F, 6 << 20),
        limit=10 << 20,
        specs=[SMEM, ANY, VMEM, VMEM, VMEM],
        scratch=[
            pltpu.VMEM((CORE * ZL, BS, F), bf16),
            pltpu.VMEM((X * Y, SLOTS, BS, BS), bf16),
            pltpu.SemaphoreType.DMA((X * Y,)),
        ],
    )
    four = jax.ShapeDtypeStruct((Y, 2, BS, F), bf16)
    one = jax.ShapeDtypeStruct((BS, F), bf16)
    staged = whole(stage_kernel, [exchange(terms, True)], four, "stage", (0, 3 << 20))
    parts = exchange(staged, False)
    send = whole(send_kernel, [parts], one, "send", (0, 1 << 18))
    other = lax.ppermute(send, "zh", [(0, 1), (1, 0)])
    return whole(
        finish_kernel,
        [parts, other, weight, out_bias[None]],
        one,
        "finish",
        (2 * BS * F * F, 1 << 19),
    )


def solution(mesh):
    fine = Mesh(
        mesh.devices.reshape(ZL, CORE, X, Y, ZH), ("zl", "core", "x", "y", "zh")
    )
    row, col = ("zl", "core"), ("x", "y", "zh")
    return jax.shard_map(
        local,
        mesh=fine,
        in_specs=(
            P(row + col, None),
            P(row, col, None, None),
            P(row, col),
            P(row, col),
            P(),
            P(),
        ),
        out_specs=P(row + col, None),
        check_vma=False,
    )
```

```python
import jax
import jax.numpy as jnp
from jax import lax
from jax.experimental import pallas as pl
from jax.experimental.pallas import tpu as pltpu
from jax.sharding import Mesh, PartitionSpec as P

ZL, CORE, X, Y, ZH = 8, 2, 4, 4, 2
SLOTS, BS, F = 4, 128, 256
COUNT, HALF = SLOTS, SLOTS + 1
VMEM = pl.BlockSpec(memory_space=pltpu.VMEM)
SMEM = pl.BlockSpec(memory_space=pltpu.SMEM)
ANY = pl.BlockSpec(memory_space=pl.ANY)


def whole(
    kernel,
    ins,
    out_shape,
    name,
    cost,
    limit=4 << 20,
    specs=None,
    out_specs=None,
    scratch=(),
):
    return pl.pallas_call(
        kernel,
        in_specs=specs or [VMEM] * len(ins),
        out_specs=out_specs or jax.tree.map(lambda _: VMEM, out_shape),
        out_shape=out_shape,
        scratch_shapes=scratch,
        compiler_params=pltpu.CompilerParams(vmem_limit_bytes=limit),
        cost_estimate=pl.CostEstimate(
            flops=cost[0], bytes_accessed=cost[1], transcendentals=0
        ),
        name=name,
    )(*ins)


def copy_kernel(in_ref, out_ref):
    out_ref[...] = in_ref[...]


def side_by_side(table_ref, row, block_of):
    count = table_ref[COUNT, row]
    lhs = []
    for k in range(SLOTS):
        block = block_of(k)
        lhs.append(jnp.where(k < count, block, jnp.zeros_like(block)))
    return jnp.concatenate(lhs, axis=1)


def product(table_ref, row, lhs, stripe_ref):
    rhs = [stripe_ref[table_ref[k, row]] for k in range(SLOTS)]
    term = jnp.dot(
        lhs, jnp.concatenate(rhs, axis=0), preferred_element_type=jnp.float32
    )
    return term.astype(jnp.bfloat16)


def far_lhs_kernel(table_ref, blocks_ref, out_ref):
    step = blocks_ref.shape[0]
    base = pl.program_id(0) * step
    for i in range(step):
        row = 2 * (base + i) + 1 - table_ref[HALF, 0]
        out_ref[i] = side_by_side(table_ref, row, lambda k: blocks_ref[i, 0, k])


def far_lhs_rows(table, blocks):
    step = 4
    return pl.pallas_call(
        far_lhs_kernel,
        grid_spec=pltpu.PrefetchScalarGridSpec(
            num_scalar_prefetch=1,
            grid=(X * Y // step,),
            in_specs=[
                pl.BlockSpec(
                    (step, 1, SLOTS, BS, BS),
                    lambda i, table_ref: (i, 1 - table_ref[HALF, 0], 0, 0, 0),
                )
            ],
            out_specs=pl.BlockSpec((step, BS, SLOTS * BS), lambda i, *_: (i, 0, 0)),
        ),
        out_shape=jax.ShapeDtypeStruct((X * Y, BS, SLOTS * BS), jnp.bfloat16),
        compiler_params=pltpu.CompilerParams(vmem_limit_bytes=6 << 20),
        cost_estimate=pl.CostEstimate(
            flops=0, bytes_accessed=4 << 20, transcendentals=0
        ),
        name="far_lhs",
    )(table, blocks)


def far_kernel(
    table_ref, lhs_ref, near_ref, across_ref, stripe_ref, out_ref, made, sem
):
    stripe_ref[:ZL] = near_ref[...]
    stripe_ref[ZL:] = across_ref[...]
    group = X * Y // sem.shape[0]
    stores = []
    for g in range(sem.shape[0]):
        for j in range(g * group, (g + 1) * group):
            made[j] = product(
                table_ref, 2 * j + 1 - table_ref[HALF, 0], lhs_ref[j], stripe_ref
            )
        part = pl.ds(g * group, group)
        stores.append(
            pltpu.make_async_copy(made.at[part], out_ref.at[part], sem.at[g])
        )
        stores[-1].start()
    for store in stores:
        store.wait()


def near_kernel(table_ref, blocks_ref, stripe_ref, out_ref):
    step = blocks_ref.shape[0]
    base = pl.program_id(0) * step
    for i in range(step):
        row = 2 * (base + i) + table_ref[HALF, 0]
        lhs = side_by_side(table_ref, row, lambda k: blocks_ref[i, 0, k])
        out_ref[i] = product(table_ref, row, lhs, stripe_ref)


def near_half(table, blocks, stripe):
    step = 4
    return pl.pallas_call(
        near_kernel,
        grid_spec=pltpu.PrefetchScalarGridSpec(
            num_scalar_prefetch=1,
            grid=(X * Y // step,),
            in_specs=[
                pl.BlockSpec(
                    (step, 1, SLOTS, BS, BS),
                    lambda i, table_ref: (i, table_ref[HALF, 0], 0, 0, 0),
                ),
                VMEM,
            ],
            out_specs=pl.BlockSpec((step, BS, F), lambda i, *_: (i, 0, 0)),
        ),
        out_shape=jax.ShapeDtypeStruct((X * Y, BS, F), jnp.bfloat16),
        compiler_params=pltpu.CompilerParams(vmem_limit_bytes=8 << 20),
        cost_estimate=pl.CostEstimate(
            flops=2 * X * Y * SLOTS * BS * BS * F,
            bytes_accessed=4 << 20,
            transcendentals=0,
        ),
        name="near_terms",
    )(table, blocks, stripe)


def total(parts):
    acc = parts[0].astype(jnp.float32)
    for part in parts[1:]:
        acc = acc + part.astype(jnp.float32)
    return acc


def send_kernel(parts_ref, out_ref):
    out_ref[...] = total([parts_ref[k] for k in range(X * Y)]).astype(jnp.bfloat16)


def finish_kernel(parts_ref, other_ref, weight_ref, bias_ref, out_ref):
    summed = total([parts_ref[k] for k in range(X * Y)]) + other_ref[...].astype(
        jnp.float32
    )
    hidden = jnp.dot(
        summed.astype(jnp.bfloat16),
        weight_ref[...],
        preferred_element_type=jnp.float32,
    )
    out_ref[...] = jnp.maximum(hidden + bias_ref[...], 0.0).astype(jnp.bfloat16)


def shard_table(block_col, row_count):
    zl, core, zh = (
        lax.axis_index(a).astype(jnp.int32) for a in ("zl", "core", "zh")
    )
    offset = block_col.T ^ (CORE * zl + core)
    spots = (
        ((offset >> 3) & 1)
        | ((offset >> 1) & 2)
        | ((offset << 1) & 4)
        | ((offset << 3) & 8)
    )
    counts = row_count.T
    return jnp.concatenate([spots, counts, jnp.full_like(counts, zh)], axis=0)


def local(features, blocks, block_col, row_count, weight, out_bias):
    bf16 = jnp.bfloat16
    table = shard_table(block_col, row_count)
    blocks = pltpu.with_memory_space_constraint(
        blocks.reshape(X * Y, ZH, SLOTS, BS, BS), pltpu.HBM
    )
    own = whole(
        copy_kernel,
        [features[None]],
        jax.ShapeDtypeStruct((1, BS, F), bf16),
        "own",
        (0, 1 << 17),
    )
    held = own
    for bit in (4, 2, 1):
        came = lax.ppermute(
            features[None] if bit == 4 else held,
            "zl",
            [(z, z ^ bit) for z in range(ZL)],
        )
        if bit == 4:
            came, table = lax.optimization_barrier((came, table))
            far_lhs = far_lhs_rows(table, blocks)
        if bit == 2:
            came, far_lhs = lax.optimization_barrier((came, far_lhs))
        held = jnp.concatenate([held, came], axis=0)
    across = lax.ppermute(held, "core", [(0, 1), (1, 0)])
    half = (X * Y, BS, F)
    one = jax.ShapeDtypeStruct((BS, F), bf16)
    stripe, far_terms = whole(
        far_kernel,
        [table, far_lhs, held, across],
        [jax.ShapeDtypeStruct(half, bf16)] * 2,
        "far_terms",
        (2 * X * Y * SLOTS * BS * BS * F, 4 << 20),
        limit=8 << 20,
        specs=[SMEM, VMEM, VMEM, VMEM],
        out_specs=[VMEM, ANY],
        scratch=[pltpu.VMEM(half, bf16), pltpu.SemaphoreType.DMA((4,))],
    )
    near_terms = near_half(table, blocks, stripe)
    far_parts = lax.all_to_all(far_terms, ("x", "y"), 0, 0)
    near_parts = lax.all_to_all(near_terms, ("x", "y"), 0, 0)
    send = whole(send_kernel, [far_parts], one, "send", (0, 1 << 20))
    other = lax.ppermute(send, "zh", [(0, 1), (1, 0)])
    return whole(
        finish_kernel,
        [near_parts, other, weight, out_bias[None]],
        one,
        "finish",
        (2 * BS * F * F, 2 << 20),
    )


def solution(mesh):
    fine = Mesh(
        mesh.devices.reshape(ZL, CORE, X, Y, ZH), ("zl", "core", "x", "y", "zh")
    )
    row, col = ("zl", "core"), ("x", "y", "zh")
    return jax.shard_map(
        local,
        mesh=fine,
        in_specs=(
            P(row + col, None),
            P(row, col, None, None),
            P(row, col),
            P(row, col),
            P(),
            P(),
        ),
        out_specs=P(row + col, None),
        check_vma=False,
    )
```

```python
import jax
import jax.numpy as jnp
from jax import lax
from jax.experimental import pallas as pl
from jax.experimental.pallas import tpu as pltpu
from jax.sharding import Mesh, PartitionSpec as P

ZL, CORE, X, Y, ZH = 8, 2, 4, 4, 2
SLOTS, BS, F = 4, 128, 256
COUNT, HALF, SIDE, PLACE = range(SLOTS, SLOTS + 4)
VMEM = pl.BlockSpec(memory_space=pltpu.VMEM)
SMEM = pl.BlockSpec(memory_space=pltpu.SMEM)
ANY = pl.BlockSpec(memory_space=pl.ANY)


def whole(
    kernel,
    ins,
    out_shape,
    name,
    cost,
    limit=4 << 20,
    specs=None,
    out_specs=None,
    scratch=(),
):
    return pl.pallas_call(
        kernel,
        in_specs=specs or [VMEM] * len(ins),
        out_specs=out_specs or jax.tree.map(lambda _: VMEM, out_shape),
        out_shape=out_shape,
        scratch_shapes=scratch,
        compiler_params=pltpu.CompilerParams(vmem_limit_bytes=limit),
        cost_estimate=pl.CostEstimate(
            flops=cost[0], bytes_accessed=cost[1], transcendentals=0
        ),
        name=name,
    )(*ins)


def copy_kernel(in_ref, out_ref):
    out_ref[...] = in_ref[...]


def side_by_side(table_ref, row, block_of):
    count = table_ref[COUNT, row]
    lhs = []
    for k in range(SLOTS):
        block = block_of(k)
        lhs.append(jnp.where(k < count, block, jnp.zeros_like(block)))
    return jnp.concatenate(lhs, axis=1)


def product(table_ref, row, lhs, stripe_ref):
    rhs = [stripe_ref[table_ref[k, row]] for k in range(SLOTS)]
    term = jnp.dot(
        lhs, jnp.concatenate(rhs, axis=0), preferred_element_type=jnp.float32
    )
    return term.astype(jnp.bfloat16)


def far_lhs_kernel(table_ref, blocks_ref, out_ref):
    step = blocks_ref.shape[0]
    base = pl.program_id(0) * step
    for i in range(step):
        row = 2 * (base + i) + 1 - table_ref[HALF, 0]
        out_ref[i] = side_by_side(table_ref, row, lambda k: blocks_ref[i, 0, k])


def far_lhs_rows(table, blocks):
    step = 4
    return pl.pallas_call(
        far_lhs_kernel,
        grid_spec=pltpu.PrefetchScalarGridSpec(
            num_scalar_prefetch=1,
            grid=(X * Y // step,),
            in_specs=[
                pl.BlockSpec(
                    (step, 1, SLOTS, BS, BS),
                    lambda i, table_ref: (i, 1 - table_ref[HALF, 0], 0, 0, 0),
                )
            ],
            out_specs=pl.BlockSpec((step, BS, SLOTS * BS), lambda i, *_: (i, 0, 0)),
        ),
        out_shape=jax.ShapeDtypeStruct((X * Y, BS, SLOTS * BS), jnp.bfloat16),
        compiler_params=pltpu.CompilerParams(vmem_limit_bytes=6 << 20),
        cost_estimate=pl.CostEstimate(
            flops=0, bytes_accessed=4 << 20, transcendentals=0
        ),
        name="far_lhs",
    )(table, blocks)


def far_kernel(
    table_ref, lhs_ref, near_ref, across_ref, stripe_ref, out_ref, made, sem
):
    stripe_ref[:ZL] = near_ref[...]
    stripe_ref[ZL:] = across_ref[...]
    group = X * Y // sem.shape[0]
    stores = []
    for g in range(sem.shape[0]):
        for j in range(g * group, (g + 1) * group):
            made[j] = product(
                table_ref, 2 * j + 1 - table_ref[HALF, 0], lhs_ref[j], stripe_ref
            )
        part = pl.ds(g * group, group)
        stores.append(
            pltpu.make_async_copy(made.at[part], out_ref.at[part], sem.at[g])
        )
        stores[-1].start()
    for store in stores:
        store.wait()


def near_kernel(table_ref, blocks_ref, stripe_ref, *refs):
    outs, (held, sem) = refs[:X], refs[X:]
    zh, side, place = (table_ref[i, 0] for i in (HALF, SIDE, PLACE))
    loads = [
        pltpu.make_async_copy(blocks_ref.at[j, zh], held.at[j], sem.at[j])
        for j in range(X * Y)
    ]
    for load in loads:
        load.start()
    for load in loads:
        load.wait()
    for d in range(X):
        k = (place + d) % X
        for m in range(Y):
            j = jnp.where(side == 0, k * Y + m, m * Y + k)
            row = 2 * j + zh
            lhs = side_by_side(table_ref, row, lambda s: held[j, s])
            outs[d][m] = product(table_ref, row, lhs, stripe_ref)


def total(parts):
    acc = parts[0].astype(jnp.float32)
    for part in parts[1:]:
        acc = acc + part.astype(jnp.float32)
    return acc


def send_kernel(parts_ref, out_ref):
    out_ref[...] = total([parts_ref[k] for k in range(X * Y)]).astype(jnp.bfloat16)


def near_sum_kernel(*refs):
    parts, out_ref = refs[:-1], refs[-1]
    for m in range(Y):
        out_ref[m] = total([part[m] for part in parts]).astype(jnp.bfloat16)


def widen_kernel(in_ref, out_ref):
    out_ref[...] = in_ref[...].astype(jnp.float32)


def finish_kernel(parts_ref, other_ref, weight_ref, bias_ref, out_ref):
    summed = total([parts_ref[k] for k in range(Y)]) + other_ref[...]
    hidden = jnp.dot(
        summed.astype(jnp.bfloat16),
        weight_ref[...],
        preferred_element_type=jnp.float32,
    )
    out_ref[...] = jnp.maximum(hidden + bias_ref[...], 0.0).astype(jnp.bfloat16)


def shard_table(block_col, row_count):
    zl, core, zh = (
        lax.axis_index(a).astype(jnp.int32) for a in ("zl", "core", "zh")
    )
    offset = block_col.T ^ (CORE * zl + core)
    spots = (
        ((offset >> 3) & 1)
        | ((offset >> 1) & 2)
        | ((offset << 1) & 4)
        | ((offset << 3) & 8)
    )
    counts = row_count.T
    place = jnp.where(core == 0, lax.axis_index("x"), lax.axis_index("y"))
    return jnp.concatenate(
        [spots, counts] + [jnp.full_like(counts, v) for v in (zh, core, place)], axis=0
    )


def along(first):
    by_x = [[x * Y + y for x in range(X)] for y in range(Y)]
    by_y = [[x * Y + y for y in range(Y)] for x in range(X)]
    sides = (by_x, by_y) if first else (by_y, by_x)
    return [[c * X * Y + i for i in g] for c, gs in enumerate(sides) for g in gs]


def pass_on(value, d):
    pairs = [(g[i], g[(i + d) % X]) for g in along(True) for i in range(X)]
    return lax.ppermute(value, ("core", "x", "y"), pairs)


def local(features, blocks, block_col, row_count, weight, out_bias):
    bf16 = jnp.bfloat16
    table = shard_table(block_col, row_count)
    blocks = pltpu.with_memory_space_constraint(
        blocks.reshape(X * Y, ZH, SLOTS, BS, BS), pltpu.HBM
    )
    own = whole(
        copy_kernel,
        [features[None]],
        jax.ShapeDtypeStruct((1, BS, F), bf16),
        "own",
        (0, 1 << 17),
    )
    held = own
    for bit in (4, 2, 1):
        came = lax.ppermute(
            features[None] if bit == 4 else held,
            "zl",
            [(z, z ^ bit) for z in range(ZL)],
        )
        if bit == 4:
            came, table = lax.optimization_barrier((came, table))
            far_lhs = far_lhs_rows(table, blocks)
        if bit == 2:
            came, far_lhs = lax.optimization_barrier((came, far_lhs))
        held = jnp.concatenate([held, came], axis=0)
    across = lax.ppermute(held, "core", [(0, 1), (1, 0)])
    half = (X * Y, BS, F)
    one = jax.ShapeDtypeStruct((BS, F), bf16)
    stripe, far_terms = whole(
        far_kernel,
        [table, far_lhs, held, across],
        [jax.ShapeDtypeStruct(half, bf16)] * 2,
        "far_terms",
        (2 * X * Y * SLOTS * BS * BS * F, 4 << 20),
        limit=8 << 20,
        specs=[SMEM, VMEM, VMEM, VMEM],
        out_specs=[VMEM, ANY],
        scratch=[pltpu.VMEM(half, bf16), pltpu.SemaphoreType.DMA((4,))],
    )
    far_parts = lax.all_to_all(far_terms, ("x", "y"), 0, 0)
    quarter = jax.ShapeDtypeStruct((Y, BS, F), bf16)
    near_terms = whole(
        near_kernel,
        [table, blocks, stripe],
        [quarter] * X,
        "near_terms",
        (2 * X * Y * SLOTS * BS * BS * F, 4 << 20),
        limit=6 << 20,
        specs=[SMEM, ANY, VMEM],
        scratch=[
            pltpu.VMEM((X * Y, SLOTS, BS, BS), bf16),
            pltpu.SemaphoreType.DMA((X * Y,)),
        ],
    )
    near = [near_terms[0]] + [pass_on(near_terms[d], d) for d in range(1, X)]
    send = whole(send_kernel, [far_parts], one, "send", (0, 1 << 20))
    other = lax.ppermute(send, "zh", [(0, 1), (1, 0)])
    near = whole(near_sum_kernel, near, quarter, "near_sum", (0, 1 << 20))
    near_parts = lax.all_to_all(
        near, ("core", "x", "y"), 0, 0, axis_index_groups=along(False)
    )
    other = whole(
        widen_kernel,
        [other],
        jax.ShapeDtypeStruct((BS, F), jnp.float32),
        "widen",
        (1 << 35, 1 << 26),
    )
    return whole(
        finish_kernel,
        [near_parts, other, weight, out_bias[None]],
        one,
        "finish",
        (2 * BS * F * F, 2 << 20),
    )


def solution(mesh):
    fine = Mesh(
        mesh.devices.reshape(ZL, CORE, X, Y, ZH), ("zl", "core", "x", "y", "zh")
    )
    row, col = ("zl", "core"), ("x", "y", "zh")
    return jax.shard_map(
        local,
        mesh=fine,
        in_specs=(
            P(row + col, None),
            P(row, col, None, None),
            P(row, col),
            P(row, col),
            P(),
            P(),
        ),
        out_specs=P(row + col, None),
        check_vma=False,
    )
```

```python
import jax
import jax.numpy as jnp
from jax import lax
from jax.experimental import pallas as pl
from jax.experimental.pallas import tpu as pltpu
from jax.sharding import Mesh, PartitionSpec as P

ZL, CORE, X, Y, ZH = 8, 2, 4, 4, 2
SLOTS, BS, F = 4, 128, 256
COUNT, HALF, SIDE, PLACE = range(SLOTS, SLOTS + 4)
VMEM = pl.BlockSpec(memory_space=pltpu.VMEM)
SMEM = pl.BlockSpec(memory_space=pltpu.SMEM)
ANY = pl.BlockSpec(memory_space=pl.ANY)


def whole(
    kernel,
    ins,
    out_shape,
    name,
    cost,
    limit=4 << 20,
    specs=None,
    out_specs=None,
    scratch=(),
):
    return pl.pallas_call(
        kernel,
        in_specs=specs or [VMEM] * len(ins),
        out_specs=out_specs or jax.tree.map(lambda _: VMEM, out_shape),
        out_shape=out_shape,
        scratch_shapes=scratch,
        compiler_params=pltpu.CompilerParams(vmem_limit_bytes=limit),
        cost_estimate=pl.CostEstimate(
            flops=cost[0], bytes_accessed=cost[1], transcendentals=0
        ),
        name=name,
    )(*ins)


def copy_kernel(in_ref, out_ref):
    out_ref[...] = in_ref[...]


def side_by_side(table_ref, row, block_of):
    count = table_ref[COUNT, row]
    lhs = []
    for k in range(SLOTS):
        block = block_of(k)
        lhs.append(jnp.where(k < count, block, jnp.zeros_like(block)))
    return jnp.concatenate(lhs, axis=1)


def product(table_ref, row, lhs, stripe_ref):
    rhs = [stripe_ref[table_ref[k, row]] for k in range(SLOTS)]
    term = jnp.dot(
        lhs, jnp.concatenate(rhs, axis=0), preferred_element_type=jnp.float32
    )
    return term.astype(jnp.bfloat16)


def far_lhs_kernel(table_ref, blocks_ref, out_ref):
    step = blocks_ref.shape[0]
    base = pl.program_id(0) * step
    for i in range(step):
        row = 2 * (base + i) + 1 - table_ref[HALF, 0]
        out_ref[i] = side_by_side(table_ref, row, lambda k: blocks_ref[i, 0, k])


def far_lhs_rows(table, blocks):
    step = 4
    return pl.pallas_call(
        far_lhs_kernel,
        grid_spec=pltpu.PrefetchScalarGridSpec(
            num_scalar_prefetch=1,
            grid=(X * Y // step,),
            in_specs=[
                pl.BlockSpec(
                    (step, 1, SLOTS, BS, BS),
                    lambda i, table_ref: (i, 1 - table_ref[HALF, 0], 0, 0, 0),
                )
            ],
            out_specs=pl.BlockSpec((step, BS, SLOTS * BS), lambda i, *_: (i, 0, 0)),
        ),
        out_shape=jax.ShapeDtypeStruct((X * Y, BS, SLOTS * BS), jnp.bfloat16),
        compiler_params=pltpu.CompilerParams(vmem_limit_bytes=6 << 20),
        cost_estimate=pl.CostEstimate(
            flops=0, bytes_accessed=4 << 20, transcendentals=0
        ),
        name="far_lhs",
    )(table, blocks)


def far_kernel(table_ref, lhs_ref, *refs):
    trio, p6, ones, p7, core0, core1 = refs[:6]
    stripe_ref, out_ref, made, sem = refs[6:]
    near = {0: trio.at[0], 4: trio.at[1], 2: trio.at[2], 6: p6.at[0]}
    near |= {1: ones.at[0], 5: ones.at[1], 3: ones.at[2], 7: p7.at[0]}
    across = {d: core0.at[i] for i, d in enumerate((0, 4, 2, 6))}
    across |= {d: core1.at[i] for i, d in enumerate((1, 5, 3, 7))}
    for d in range(ZL):
        stripe_ref[CORE * d] = near[d][...]
        stripe_ref[CORE * d + 1] = across[d][...]
    group = X * Y // sem.shape[0]
    stores = []
    for g in range(sem.shape[0]):
        for j in range(g * group, (g + 1) * group):
            made[j] = product(
                table_ref, 2 * j + 1 - table_ref[HALF, 0], lhs_ref[j], stripe_ref
            )
        part = pl.ds(g * group, group)
        stores.append(
            pltpu.make_async_copy(made.at[part], out_ref.at[part], sem.at[g])
        )
        stores[-1].start()
    for store in stores:
        store.wait()


def near_kernel(table_ref, blocks_ref, stripe_ref, *refs):
    outs, (held, sem) = refs[:X], refs[X:]
    zh, side, place = (table_ref[i, 0] for i in (HALF, SIDE, PLACE))
    loads = [
        pltpu.make_async_copy(blocks_ref.at[j, zh], held.at[j], sem.at[j])
        for j in range(X * Y)
    ]
    for load in loads:
        load.start()
    for load in loads:
        load.wait()
    for d in range(X):
        k = (place + d) % X
        for m in range(Y):
            j = jnp.where(side == 0, k * Y + m, m * Y + k)
            row = 2 * j + zh
            lhs = side_by_side(table_ref, row, lambda s: held[j, s])
            outs[d][m] = product(table_ref, row, lhs, stripe_ref)


def total(parts):
    acc = parts[0].astype(jnp.float32)
    for part in parts[1:]:
        acc = acc + part.astype(jnp.float32)
    return acc


def send_kernel(parts_ref, out_ref):
    out_ref[...] = total([parts_ref[k] for k in range(X * Y)]).astype(jnp.bfloat16)


def near_sum_kernel(*refs):
    parts, out_ref = refs[:-1], refs[-1]
    for m in range(Y):
        out_ref[m] = total([part[m] for part in parts]).astype(jnp.bfloat16)


def finish_kernel(parts_ref, other_ref, weight_ref, bias_ref, out_ref):
    summed = total([parts_ref[k] for k in range(Y)]) + other_ref[...].astype(
        jnp.float32
    )
    hidden = jnp.dot(
        summed.astype(jnp.bfloat16),
        weight_ref[...],
        preferred_element_type=jnp.float32,
    )
    out_ref[...] = jnp.maximum(hidden + bias_ref[...], 0.0).astype(jnp.bfloat16)


def shard_table(block_col, row_count):
    zl, core, zh = (
        lax.axis_index(a).astype(jnp.int32) for a in ("zl", "core", "zh")
    )
    spots = block_col.T ^ (CORE * zl + core)
    counts = row_count.T
    place = jnp.where(core == 0, lax.axis_index("x"), lax.axis_index("y"))
    return jnp.concatenate(
        [spots, counts] + [jnp.full_like(counts, v) for v in (zh, core, place)], axis=0
    )


def along(first):
    by_x = [[x * Y + y for x in range(X)] for y in range(Y)]
    by_y = [[x * Y + y for y in range(Y)] for x in range(X)]
    sides = (by_x, by_y) if first else (by_y, by_x)
    return [[c * X * Y + i for i in g] for c, gs in enumerate(sides) for g in gs]


def pass_on(value, d):
    pairs = [(g[i], g[(i + d) % X]) for g in along(True) for i in range(X)]
    return lax.ppermute(value, ("core", "x", "y"), pairs)


def local(features, blocks, block_col, row_count, weight, out_bias):
    bf16 = jnp.bfloat16
    table = shard_table(block_col, row_count)
    blocks = pltpu.with_memory_space_constraint(
        blocks.reshape(X * Y, ZH, SLOTS, BS, BS), pltpu.HBM
    )
    own = whole(
        copy_kernel,
        [features[None]],
        jax.ShapeDtypeStruct((1, BS, F), bf16),
        "own",
        (0, 1 << 17),
    )
    def hop(value, bit):
        return lax.ppermute(value, "zl", [(z, z ^ bit) for z in range(ZL)])

    def cross(value):
        return lax.ppermute(value, "core", [(0, 1), (1, 0)])

    p4, p2 = hop(features[None], 4), hop(features[None], 2)
    p4, table = lax.optimization_barrier((p4, table))
    p6 = hop(p4, 2)
    far_lhs = far_lhs_rows(table, blocks)
    trio = jnp.concatenate([own, p4, p2], axis=0)
    ones = hop(trio, 1)
    p6, far_lhs = lax.optimization_barrier((p6, far_lhs))
    p7 = hop(p6, 1)
    core0 = cross(jnp.concatenate([trio, p6], axis=0))
    core1 = cross(jnp.concatenate([ones, p7], axis=0))
    half = (X * Y, BS, F)
    one = jax.ShapeDtypeStruct((BS, F), bf16)
    stripe, far_terms = whole(
        far_kernel,
        [table, far_lhs, trio, p6, ones, p7, core0, core1],
        [jax.ShapeDtypeStruct(half, bf16)] * 2,
        "far_terms",
        (2 * X * Y * SLOTS * BS * BS * F, 4 << 20),
        limit=8 << 20,
        specs=[SMEM] + [VMEM] * 7,
        out_specs=[VMEM, ANY],
        scratch=[pltpu.VMEM(half, bf16), pltpu.SemaphoreType.DMA((4,))],
    )
    far_parts = lax.all_to_all(far_terms, ("x", "y"), 0, 0)
    quarter = jax.ShapeDtypeStruct((Y, BS, F), bf16)
    near_terms = whole(
        near_kernel,
        [table, blocks, stripe],
        [quarter] * X,
        "near_terms",
        (2 * X * Y * SLOTS * BS * BS * F, 4 << 20),
        limit=6 << 20,
        specs=[SMEM, ANY, VMEM],
        scratch=[
            pltpu.VMEM((X * Y, SLOTS, BS, BS), bf16),
            pltpu.SemaphoreType.DMA((X * Y,)),
        ],
    )
    near = [near_terms[0]] + [pass_on(near_terms[d], d) for d in range(1, X)]
    send = whole(send_kernel, [far_parts], one, "send", (0, 1 << 20))
    other = lax.ppermute(send, "zh", [(0, 1), (1, 0)])
    near = whole(near_sum_kernel, near, quarter, "near_sum", (0, 1 << 20))
    near_parts = lax.all_to_all(
        near, ("core", "x", "y"), 0, 0, axis_index_groups=along(False)
    )
    return whole(
        finish_kernel,
        [near_parts, other, weight, out_bias[None]],
        one,
        "finish",
        (2 * BS * F * F, 2 << 20),
    )


def solution(mesh):
    fine = Mesh(
        mesh.devices.reshape(ZL, CORE, X, Y, ZH), ("zl", "core", "x", "y", "zh")
    )
    row, col = ("zl", "core"), ("x", "y", "zh")
    return jax.shard_map(
        local,
        mesh=fine,
        in_specs=(
            P(row + col, None),
            P(row, col, None, None),
            P(row, col),
            P(row, col),
            P(),
            P(),
        ),
        out_specs=P(row + col, None),
        check_vma=False,
    )
```

```python
import jax
import jax.numpy as jnp
from jax import lax
from jax.experimental import pallas as pl
from jax.experimental.pallas import tpu as pltpu
from jax.sharding import Mesh, PartitionSpec as P

ZL, CORE, X, Y, ZH = 8, 2, 4, 4, 2
SLOTS, BS, F = 4, 128, 256
COUNT, HALF = SLOTS, SLOTS + 1
LONG = (1 << 35, 1 << 26)
VMEM = pl.BlockSpec(memory_space=pltpu.VMEM)
SMEM = pl.BlockSpec(memory_space=pltpu.SMEM)
ANY = pl.BlockSpec(memory_space=pl.ANY)


def whole(
    kernel,
    ins,
    out_shape,
    name,
    cost,
    limit=4 << 20,
    specs=None,
    out_specs=None,
    scratch=(),
):
    return pl.pallas_call(
        kernel,
        in_specs=specs or [VMEM] * len(ins),
        out_specs=out_specs or jax.tree.map(lambda _: VMEM, out_shape),
        out_shape=out_shape,
        scratch_shapes=scratch,
        compiler_params=pltpu.CompilerParams(vmem_limit_bytes=limit),
        cost_estimate=pl.CostEstimate(
            flops=cost[0], bytes_accessed=cost[1], transcendentals=0
        ),
        name=name,
    )(*ins)


def copy_kernel(in_ref, out_ref):
    out_ref[...] = in_ref[...]


def side_by_side(table_ref, row, block_of):
    count = table_ref[COUNT, row]
    lhs = []
    for k in range(SLOTS):
        block = block_of(k)
        lhs.append(jnp.where(k < count, block, jnp.zeros_like(block)))
    return jnp.concatenate(lhs, axis=1)


def product(table_ref, row, lhs, stripe_ref):
    rhs = [stripe_ref[table_ref[k, row]] for k in range(SLOTS)]
    term = jnp.dot(
        lhs, jnp.concatenate(rhs, axis=0), preferred_element_type=jnp.float32
    )
    return term.astype(jnp.bfloat16)


def far_lhs_kernel(table_ref, blocks_ref, out_ref):
    step = blocks_ref.shape[0]
    base = pl.program_id(0) * step
    for i in range(step):
        row = 2 * (base + i) + 1 - table_ref[HALF, 0]
        out_ref[i] = side_by_side(table_ref, row, lambda k: blocks_ref[i, 0, k])


def far_lhs_rows(table, blocks):
    step = 4
    return pl.pallas_call(
        far_lhs_kernel,
        grid_spec=pltpu.PrefetchScalarGridSpec(
            num_scalar_prefetch=1,
            grid=(X * Y // step,),
            in_specs=[
                pl.BlockSpec(
                    (step, 1, SLOTS, BS, BS),
                    lambda i, table_ref: (i, 1 - table_ref[HALF, 0], 0, 0, 0),
                )
            ],
            out_specs=pl.BlockSpec((step, BS, SLOTS * BS), lambda i, *_: (i, 0, 0)),
        ),
        out_shape=jax.ShapeDtypeStruct((X * Y, BS, SLOTS * BS), jnp.bfloat16),
        compiler_params=pltpu.CompilerParams(vmem_limit_bytes=6 << 20),
        cost_estimate=pl.CostEstimate(
            flops=0, bytes_accessed=4 << 20, transcendentals=0
        ),
        name="far_lhs",
    )(table, blocks)


def far_kernel(table_ref, lhs_ref, *refs):
    trio, p6, ones, p7, core0, core1 = refs[:6]
    stripe_ref, out_ref, made, sem = refs[6:]
    near = {0: trio.at[0], 4: trio.at[1], 2: trio.at[2], 6: p6.at[0]}
    near |= {1: ones.at[0], 5: ones.at[1], 3: ones.at[2], 7: p7.at[0]}
    across = {d: core0.at[i] for i, d in enumerate((0, 4, 2, 6))}
    across |= {d: core1.at[i] for i, d in enumerate((1, 5, 3, 7))}
    for d in range(ZL):
        stripe_ref[CORE * d] = near[d][...]
        stripe_ref[CORE * d + 1] = across[d][...]
    group = X * Y // sem.shape[0]
    stores = []
    for g in range(sem.shape[0]):
        for j in range(g * group, (g + 1) * group):
            made[j] = product(
                table_ref, 2 * j + 1 - table_ref[HALF, 0], lhs_ref[j], stripe_ref
            )
        part = pl.ds(g * group, group)
        stores.append(
            pltpu.make_async_copy(made.at[part], out_ref.at[part], sem.at[g])
        )
        stores[-1].start()
    for store in stores:
        store.wait()


def near_kernel(table_ref, blocks_ref, stripe_ref, out_ref):
    step = blocks_ref.shape[0]
    base = pl.program_id(0) * step
    for i in range(step):
        row = 2 * (base + i) + table_ref[HALF, 0]
        lhs = side_by_side(table_ref, row, lambda k: blocks_ref[i, 0, k])
        out_ref[i] = product(table_ref, row, lhs, stripe_ref)


def near_half(table, blocks, stripe):
    step = 4
    return pl.pallas_call(
        near_kernel,
        grid_spec=pltpu.PrefetchScalarGridSpec(
            num_scalar_prefetch=1,
            grid=(X * Y // step,),
            in_specs=[
                pl.BlockSpec(
                    (step, 1, SLOTS, BS, BS),
                    lambda i, table_ref: (i, table_ref[HALF, 0], 0, 0, 0),
                ),
                VMEM,
            ],
            out_specs=pl.BlockSpec((step, BS, F), lambda i, *_: (i, 0, 0)),
        ),
        out_shape=jax.ShapeDtypeStruct((X * Y, BS, F), jnp.bfloat16),
        compiler_params=pltpu.CompilerParams(vmem_limit_bytes=8 << 20),
        cost_estimate=pl.CostEstimate(
            flops=2 * X * Y * SLOTS * BS * BS * F,
            bytes_accessed=4 << 20,
            transcendentals=0,
        ),
        name="near_terms",
    )(table, blocks, stripe)


def total(parts):
    acc = parts[0].astype(jnp.float32)
    for part in parts[1:]:
        acc = acc + part.astype(jnp.float32)
    return acc


def send_kernel(parts_ref, out_ref):
    out_ref[...] = total([parts_ref[k] for k in range(X * Y)]).astype(jnp.bfloat16)


def finish_kernel(parts_ref, other_ref, weight_ref, bias_ref, out_ref):
    summed = total([parts_ref[k] for k in range(X * Y)]) + other_ref[...].astype(
        jnp.float32
    )
    hidden = jnp.dot(
        summed.astype(jnp.bfloat16),
        weight_ref[...],
        preferred_element_type=jnp.float32,
    )
    out_ref[...] = jnp.maximum(hidden + bias_ref[...], 0.0).astype(jnp.bfloat16)


def shard_table(block_col, row_count):
    zl, core, zh = (
        lax.axis_index(a).astype(jnp.int32) for a in ("zl", "core", "zh")
    )
    spots = block_col.T ^ (CORE * zl + core)
    counts = row_count.T
    return jnp.concatenate([spots, counts, jnp.full_like(counts, zh)], axis=0)


def local(features, blocks, block_col, row_count, weight, out_bias):
    bf16 = jnp.bfloat16
    table = shard_table(block_col, row_count)
    blocks = pltpu.with_memory_space_constraint(
        blocks.reshape(X * Y, ZH, SLOTS, BS, BS), pltpu.HBM
    )
    own = whole(
        copy_kernel,
        [features[None]],
        jax.ShapeDtypeStruct((1, BS, F), bf16),
        "own",
        LONG,
    )
    def hop(value, bit):
        return lax.ppermute(value, "zl", [(z, z ^ bit) for z in range(ZL)])

    def cross(value):
        return lax.ppermute(value, "core", [(0, 1), (1, 0)])

    p4, p2 = hop(features[None], 4), hop(own, 2)
    p4, table = lax.optimization_barrier((p4, table))
    p6 = hop(p4, 2)
    far_lhs = far_lhs_rows(table, blocks)
    trio = jnp.concatenate([own, p4, p2], axis=0)
    ones = hop(trio, 1)
    p6, far_lhs = lax.optimization_barrier((p6, far_lhs))
    p7 = hop(p6, 1)
    core0 = cross(jnp.concatenate([trio, p6], axis=0))
    core1 = cross(jnp.concatenate([ones, p7], axis=0))
    half = (X * Y, BS, F)
    one = jax.ShapeDtypeStruct((BS, F), bf16)
    stripe, far_terms = whole(
        far_kernel,
        [table, far_lhs, trio, p6, ones, p7, core0, core1],
        [jax.ShapeDtypeStruct(half, bf16)] * 2,
        "far_terms",
        (2 * X * Y * SLOTS * BS * BS * F, 4 << 20),
        limit=8 << 20,
        specs=[SMEM] + [VMEM] * 7,
        out_specs=[VMEM, ANY],
        scratch=[pltpu.VMEM(half, bf16), pltpu.SemaphoreType.DMA((4,))],
    )
    near_terms = near_half(table, blocks, stripe)
    far_parts = lax.all_to_all(far_terms, ("x", "y"), 0, 0)
    near_parts = lax.all_to_all(near_terms, ("x", "y"), 0, 0)
    send = whole(send_kernel, [far_parts], one, "send", (0, 1 << 20))
    other = lax.ppermute(send, "zh", [(0, 1), (1, 0)])
    return whole(
        finish_kernel,
        [near_parts, other, weight, out_bias[None]],
        one,
        "finish",
        (2 * BS * F * F, 2 << 20),
    )


def solution(mesh):
    fine = Mesh(
        mesh.devices.reshape(ZL, CORE, X, Y, ZH), ("zl", "core", "x", "y", "zh")
    )
    row, col = ("zl", "core"), ("x", "y", "zh")
    return jax.shard_map(
        local,
        mesh=fine,
        in_specs=(
            P(row + col, None),
            P(row, col, None, None),
            P(row, col),
            P(row, col),
            P(),
            P(),
        ),
        out_specs=P(row + col, None),
        check_vma=False,
    )
```

```python
import jax
import jax.numpy as jnp
from jax import lax
from jax.experimental import pallas as pl
from jax.experimental.pallas import tpu as pltpu
from jax.sharding import Mesh, PartitionSpec as P

ZL, CORE, X, Y, ZH = 8, 2, 4, 4, 2
SLOTS, BS, F = 4, 128, 256
COUNT, HALF = SLOTS, SLOTS + 1
LONG = (1 << 35, 1 << 26)
VMEM = pl.BlockSpec(memory_space=pltpu.VMEM)
SMEM = pl.BlockSpec(memory_space=pltpu.SMEM)
ANY = pl.BlockSpec(memory_space=pl.ANY)


def whole(
    kernel,
    ins,
    out_shape,
    name,
    cost,
    limit=4 << 20,
    specs=None,
    out_specs=None,
    scratch=(),
):
    return pl.pallas_call(
        kernel,
        in_specs=specs or [VMEM] * len(ins),
        out_specs=out_specs or jax.tree.map(lambda _: VMEM, out_shape),
        out_shape=out_shape,
        scratch_shapes=scratch,
        compiler_params=pltpu.CompilerParams(vmem_limit_bytes=limit),
        cost_estimate=pl.CostEstimate(
            flops=cost[0], bytes_accessed=cost[1], transcendentals=0
        ),
        name=name,
    )(*ins)


def copy_kernel(in_ref, out_ref):
    out_ref[...] = in_ref[...]


def side_by_side(table_ref, row, block_of):
    count = table_ref[COUNT, row]
    lhs = []
    for k in range(SLOTS):
        block = block_of(k)
        lhs.append(jnp.where(k < count, block, jnp.zeros_like(block)))
    return jnp.concatenate(lhs, axis=1)


def product(table_ref, row, lhs, stripe_ref):
    rhs = [stripe_ref[table_ref[k, row]] for k in range(SLOTS)]
    term = jnp.dot(
        lhs, jnp.concatenate(rhs, axis=0), preferred_element_type=jnp.float32
    )
    return term.astype(jnp.bfloat16)


def far_lhs_kernel(table_ref, blocks_ref, out_ref):
    step = blocks_ref.shape[0]
    base = pl.program_id(0) * step
    for i in range(step):
        row = 2 * (base + i) + 1 - table_ref[HALF, 0]
        out_ref[i] = side_by_side(table_ref, row, lambda k: blocks_ref[i, 0, k])


def far_lhs_rows(table, blocks):
    step = 4
    return pl.pallas_call(
        far_lhs_kernel,
        grid_spec=pltpu.PrefetchScalarGridSpec(
            num_scalar_prefetch=1,
            grid=(X * Y // step,),
            in_specs=[
                pl.BlockSpec(
                    (step, 1, SLOTS, BS, BS),
                    lambda i, table_ref: (i, 1 - table_ref[HALF, 0], 0, 0, 0),
                )
            ],
            out_specs=pl.BlockSpec((step, BS, SLOTS * BS), lambda i, *_: (i, 0, 0)),
        ),
        out_shape=jax.ShapeDtypeStruct((X * Y, BS, SLOTS * BS), jnp.bfloat16),
        compiler_params=pltpu.CompilerParams(vmem_limit_bytes=6 << 20),
        cost_estimate=pl.CostEstimate(
            flops=0, bytes_accessed=4 << 20, transcendentals=0
        ),
        name="far_lhs",
    )(table, blocks)


def far_kernel(table_ref, lhs_ref, *refs):
    held, across, stripe_ref, out_ref, made, sem = refs
    for i, d in enumerate((0, 4, 2, 6, 1, 5, 3, 7)):
        stripe_ref[CORE * d] = held[i]
        stripe_ref[CORE * d + 1] = across[i]
    group = X * Y // sem.shape[0]
    stores = []
    for g in range(sem.shape[0]):
        for j in range(g * group, (g + 1) * group):
            made[j] = product(
                table_ref, 2 * j + 1 - table_ref[HALF, 0], lhs_ref[j], stripe_ref
            )
        part = pl.ds(g * group, group)
        stores.append(
            pltpu.make_async_copy(made.at[part], out_ref.at[part], sem.at[g])
        )
        stores[-1].start()
    for store in stores:
        store.wait()


def near_kernel(table_ref, blocks_ref, stripe_ref, out_ref):
    step = blocks_ref.shape[0]
    base = pl.program_id(0) * step
    for i in range(step):
        row = 2 * (base + i) + table_ref[HALF, 0]
        lhs = side_by_side(table_ref, row, lambda k: blocks_ref[i, 0, k])
        out_ref[i] = product(table_ref, row, lhs, stripe_ref)


def near_half(table, blocks, stripe):
    step = 4
    return pl.pallas_call(
        near_kernel,
        grid_spec=pltpu.PrefetchScalarGridSpec(
            num_scalar_prefetch=1,
            grid=(X * Y // step,),
            in_specs=[
                pl.BlockSpec(
                    (step, 1, SLOTS, BS, BS),
                    lambda i, table_ref: (i, table_ref[HALF, 0], 0, 0, 0),
                ),
                VMEM,
            ],
            out_specs=pl.BlockSpec((step, BS, F), lambda i, *_: (i, 0, 0)),
        ),
        out_shape=jax.ShapeDtypeStruct((X * Y, BS, F), jnp.bfloat16),
        compiler_params=pltpu.CompilerParams(vmem_limit_bytes=8 << 20),
        cost_estimate=pl.CostEstimate(
            flops=2 * X * Y * SLOTS * BS * BS * F,
            bytes_accessed=4 << 20,
            transcendentals=0,
        ),
        name="near_terms",
    )(table, blocks, stripe)


def total(parts):
    acc = parts[0].astype(jnp.float32)
    for part in parts[1:]:
        acc = acc + part.astype(jnp.float32)
    return acc


def send_kernel(parts_ref, out_ref):
    out_ref[...] = total([parts_ref[k] for k in range(X * Y)]).astype(jnp.bfloat16)


def finish_kernel(parts_ref, other_ref, weight_ref, bias_ref, out_ref):
    summed = total([parts_ref[k] for k in range(X * Y)]) + other_ref[...].astype(
        jnp.float32
    )
    hidden = jnp.dot(
        summed.astype(jnp.bfloat16),
        weight_ref[...],
        preferred_element_type=jnp.float32,
    )
    out_ref[...] = jnp.maximum(hidden + bias_ref[...], 0.0).astype(jnp.bfloat16)


def shard_table(block_col, row_count):
    zl, core, zh = (
        lax.axis_index(a).astype(jnp.int32) for a in ("zl", "core", "zh")
    )
    spots = block_col.T ^ (CORE * zl + core)
    counts = row_count.T
    return jnp.concatenate([spots, counts, jnp.full_like(counts, zh)], axis=0)


def local(features, blocks, block_col, row_count, weight, out_bias):
    bf16 = jnp.bfloat16
    table = shard_table(block_col, row_count)
    blocks = pltpu.with_memory_space_constraint(
        blocks.reshape(X * Y, ZH, SLOTS, BS, BS), pltpu.HBM
    )
    own = whole(
        copy_kernel,
        [features[None]],
        jax.ShapeDtypeStruct((1, BS, F), bf16),
        "own",
        LONG,
    )
    def hop(value, bit):
        return lax.ppermute(value, "zl", [(z, z ^ bit) for z in range(ZL)])

    def cross(value):
        return lax.ppermute(value, "core", [(0, 1), (1, 0)])

    p4, p2 = hop(features[None], 4), hop(own, 2)
    p4, table = lax.optimization_barrier((p4, table))
    p6 = hop(p4, 2)
    far_lhs = far_lhs_rows(table, blocks)
    p6, far_lhs = lax.optimization_barrier((p6, far_lhs))
    even = jnp.concatenate([own, p4, p2, p6], axis=0)
    held = jnp.concatenate([even, hop(even, 1)], axis=0)
    across = cross(held)
    half = (X * Y, BS, F)
    one = jax.ShapeDtypeStruct((BS, F), bf16)
    stripe, far_terms = whole(
        far_kernel,
        [table, far_lhs, held, across],
        [jax.ShapeDtypeStruct(half, bf16)] * 2,
        "far_terms",
        (2 * X * Y * SLOTS * BS * BS * F, 4 << 20),
        limit=8 << 20,
        specs=[SMEM, VMEM, VMEM, VMEM],
        out_specs=[VMEM, ANY],
        scratch=[pltpu.VMEM(half, bf16), pltpu.SemaphoreType.DMA((4,))],
    )
    near_terms = near_half(table, blocks, stripe)
    far_parts = lax.all_to_all(far_terms, ("x", "y"), 0, 0)
    near_parts = lax.all_to_all(near_terms, ("x", "y"), 0, 0)
    send = whole(send_kernel, [far_parts], one, "send", (0, 1 << 20))
    other = lax.ppermute(send, "zh", [(0, 1), (1, 0)])
    return whole(
        finish_kernel,
        [near_parts, other, weight, out_bias[None]],
        one,
        "finish",
        (2 * BS * F * F, 2 << 20),
    )


def solution(mesh):
    fine = Mesh(
        mesh.devices.reshape(ZL, CORE, X, Y, ZH), ("zl", "core", "x", "y", "zh")
    )
    row, col = ("zl", "core"), ("x", "y", "zh")
    return jax.shard_map(
        local,
        mesh=fine,
        in_specs=(
            P(row + col, None),
            P(row, col, None, None),
            P(row, col),
            P(row, col),
            P(),
            P(),
        ),
        out_specs=P(row + col, None),
        check_vma=False,
    )
```

```python
import jax
import jax.numpy as jnp
from jax import lax
from jax.experimental import pallas as pl
from jax.experimental.pallas import tpu as pltpu
from jax.sharding import Mesh, PartitionSpec as P

ZL, CORE, X, Y, ZH = 8, 2, 4, 4, 2
SLOTS, BS, F = 4, 128, 256
COUNT, HALF, SIDE = range(SLOTS, SLOTS + 3)
LONG = (1 << 35, 1 << 26)
VMEM = pl.BlockSpec(memory_space=pltpu.VMEM)
SMEM = pl.BlockSpec(memory_space=pltpu.SMEM)
ANY = pl.BlockSpec(memory_space=pl.ANY)


def whole(
    kernel,
    ins,
    out_shape,
    name,
    cost,
    limit=4 << 20,
    specs=None,
    out_specs=None,
    scratch=(),
):
    return pl.pallas_call(
        kernel,
        in_specs=specs or [VMEM] * len(ins),
        out_specs=out_specs or jax.tree.map(lambda _: VMEM, out_shape),
        out_shape=out_shape,
        scratch_shapes=scratch,
        compiler_params=pltpu.CompilerParams(vmem_limit_bytes=limit),
        cost_estimate=pl.CostEstimate(
            flops=cost[0], bytes_accessed=cost[1], transcendentals=0
        ),
        name=name,
    )(*ins)


def copy_kernel(in_ref, out_ref):
    out_ref[...] = in_ref[...]


def side_by_side(table_ref, row, block_of):
    count = table_ref[COUNT, row]
    lhs = []
    for k in range(SLOTS):
        block = block_of(k)
        lhs.append(jnp.where(k < count, block, jnp.zeros_like(block)))
    return jnp.concatenate(lhs, axis=1)


def product(table_ref, row, lhs, stripe_ref):
    rhs = [stripe_ref[table_ref[k, row]] for k in range(SLOTS)]
    term = jnp.dot(
        lhs, jnp.concatenate(rhs, axis=0), preferred_element_type=jnp.float32
    )
    return term.astype(jnp.bfloat16)


def far_lhs_kernel(table_ref, blocks_ref, out_ref):
    step = blocks_ref.shape[0]
    base = pl.program_id(0) * step
    for i in range(step):
        row = 2 * (base + i) + 1 - table_ref[HALF, 0]
        out_ref[i] = side_by_side(table_ref, row, lambda k: blocks_ref[i, 0, k])


def far_lhs_rows(table, blocks):
    step = 4
    return pl.pallas_call(
        far_lhs_kernel,
        grid_spec=pltpu.PrefetchScalarGridSpec(
            num_scalar_prefetch=1,
            grid=(X * Y // step,),
            in_specs=[
                pl.BlockSpec(
                    (step, 1, SLOTS, BS, BS),
                    lambda i, table_ref: (i, 1 - table_ref[HALF, 0], 0, 0, 0),
                )
            ],
            out_specs=pl.BlockSpec((step, BS, SLOTS * BS), lambda i, *_: (i, 0, 0)),
        ),
        out_shape=jax.ShapeDtypeStruct((X * Y, BS, SLOTS * BS), jnp.bfloat16),
        compiler_params=pltpu.CompilerParams(vmem_limit_bytes=6 << 20),
        cost_estimate=pl.CostEstimate(
            flops=0, bytes_accessed=4 << 20, transcendentals=0
        ),
        name="far_lhs",
    )(table, blocks)


def turned(j):
    return j % X * X + j // X


def far_kernel(table_ref, lhs_ref, *refs):
    held, across, stripe_ref, out_ref, made, sem = refs
    for i, d in enumerate((0, 4, 2, 6, 1, 5, 3, 7)):
        stripe_ref[CORE * d] = held[i]
        stripe_ref[CORE * d + 1] = across[i]
    group = X * Y // sem.shape[0]
    stores = []
    for g in range(sem.shape[0]):
        for j in range(g * group, (g + 1) * group):
            pair = jnp.where(table_ref[SIDE, 0] == 0, j, turned(j))
            row = 2 * pair + 1 - table_ref[HALF, 0]
            made[j] = product(table_ref, row, lhs_ref[pair], stripe_ref)
        part = pl.ds(g * group, group)
        stores.append(
            pltpu.make_async_copy(made.at[part], out_ref.at[part], sem.at[g])
        )
        stores[-1].start()
    for store in stores:
        store.wait()


def near_kernel(table_ref, blocks_ref, stripe_ref, out_ref):
    step = blocks_ref.shape[0]
    base = pl.program_id(0) * step
    for i in range(step):
        pair = base + i
        row = 2 * pair + table_ref[HALF, 0]
        lhs = side_by_side(table_ref, row, lambda k: blocks_ref[i, 0, k])
        spot = jnp.where(table_ref[SIDE, 0] == 0, pair, i * X + pl.program_id(0))
        out_ref[spot] = product(table_ref, row, lhs, stripe_ref)


def near_half(table, blocks, stripe):
    step = Y
    return pl.pallas_call(
        near_kernel,
        grid_spec=pltpu.PrefetchScalarGridSpec(
            num_scalar_prefetch=1,
            grid=(X * Y // step,),
            in_specs=[
                pl.BlockSpec(
                    (step, 1, SLOTS, BS, BS),
                    lambda i, table_ref: (i, table_ref[HALF, 0], 0, 0, 0),
                ),
                VMEM,
            ],
            out_specs=pl.BlockSpec((X * Y, BS, F), lambda i, *_: (0, 0, 0)),
        ),
        out_shape=jax.ShapeDtypeStruct((X * Y, BS, F), jnp.bfloat16),
        compiler_params=pltpu.CompilerParams(vmem_limit_bytes=8 << 20),
        cost_estimate=pl.CostEstimate(
            flops=2 * X * Y * SLOTS * BS * BS * F,
            bytes_accessed=4 << 20,
            transcendentals=0,
        ),
        name="near_terms",
    )(table, blocks, stripe)


def total(parts):
    acc = parts[0].astype(jnp.float32)
    for part in parts[1:]:
        acc = acc + part.astype(jnp.float32)
    return acc


def send_kernel(parts_ref, out_ref):
    out_ref[...] = total([parts_ref[k] for k in range(X * Y)]).astype(jnp.bfloat16)


def finish_kernel(parts_ref, other_ref, weight_ref, bias_ref, out_ref):
    summed = total([parts_ref[k] for k in range(X * Y)]) + other_ref[...].astype(
        jnp.float32
    )
    hidden = jnp.dot(
        summed.astype(jnp.bfloat16),
        weight_ref[...],
        preferred_element_type=jnp.float32,
    )
    out_ref[...] = jnp.maximum(hidden + bias_ref[...], 0.0).astype(jnp.bfloat16)


def shard_table(block_col, row_count):
    zl, core, zh = (
        lax.axis_index(a).astype(jnp.int32) for a in ("zl", "core", "zh")
    )
    spots = block_col.T ^ (CORE * zl + core)
    counts = row_count.T
    return jnp.concatenate(
        [spots, counts, jnp.full_like(counts, zh), jnp.full_like(counts, core)], axis=0
    )


def exchange(value):
    plane = range(X * Y)
    groups = [list(plane), [X * Y + turned(j) for j in plane]]
    return lax.all_to_all(value, ("core", "x", "y"), 0, 0, axis_index_groups=groups)


def local(features, blocks, block_col, row_count, weight, out_bias):
    bf16 = jnp.bfloat16
    table = shard_table(block_col, row_count)
    blocks = pltpu.with_memory_space_constraint(
        blocks.reshape(X * Y, ZH, SLOTS, BS, BS), pltpu.HBM
    )
    own = whole(
        copy_kernel,
        [features[None]],
        jax.ShapeDtypeStruct((1, BS, F), bf16),
        "own",
        LONG,
    )
    def hop(value, bit):
        return lax.ppermute(value, "zl", [(z, z ^ bit) for z in range(ZL)])

    def cross(value):
        return lax.ppermute(value, "core", [(0, 1), (1, 0)])

    p4, p2 = hop(features[None], 4), hop(own, 2)
    p4, table = lax.optimization_barrier((p4, table))
    p6 = hop(p4, 2)
    far_lhs = far_lhs_rows(table, blocks)
    p6, far_lhs = lax.optimization_barrier((p6, far_lhs))
    even = jnp.concatenate([own, p4, p2, p6], axis=0)
    held = jnp.concatenate([even, hop(even, 1)], axis=0)
    across = cross(held)
    half = (X * Y, BS, F)
    one = jax.ShapeDtypeStruct((BS, F), bf16)
    stripe, far_terms = whole(
        far_kernel,
        [table, far_lhs, held, across],
        [jax.ShapeDtypeStruct(half, bf16)] * 2,
        "far_terms",
        (2 * X * Y * SLOTS * BS * BS * F, 4 << 20),
        limit=8 << 20,
        specs=[SMEM, VMEM, VMEM, VMEM],
        out_specs=[VMEM, ANY],
        scratch=[pltpu.VMEM(half, bf16), pltpu.SemaphoreType.DMA((4,))],
    )
    near_terms = near_half(table, blocks, stripe)
    far_parts, near_parts = exchange(far_terms), exchange(near_terms)
    send = whole(send_kernel, [far_parts], one, "send", (0, 1 << 20))
    other = lax.ppermute(send, "zh", [(0, 1), (1, 0)])
    return whole(
        finish_kernel,
        [near_parts, other, weight, out_bias[None]],
        one,
        "finish",
        (2 * BS * F * F, 2 << 20),
    )


def solution(mesh):
    fine = Mesh(
        mesh.devices.reshape(ZL, CORE, X, Y, ZH), ("zl", "core", "x", "y", "zh")
    )
    row, col = ("zl", "core"), ("x", "y", "zh")
    return jax.shard_map(
        local,
        mesh=fine,
        in_specs=(
            P(row + col, None),
            P(row, col, None, None),
            P(row, col),
            P(row, col),
            P(),
            P(),
        ),
        out_specs=P(row + col, None),
        check_vma=False,
    )
```

```python
import jax
import jax.numpy as jnp
from jax import lax
from jax.experimental import pallas as pl
from jax.experimental.pallas import tpu as pltpu
from jax.sharding import Mesh, PartitionSpec as P

ZL, CORE, X, Y, ZH = 8, 2, 4, 4, 2
SLOTS, BS, F = 4, 128, 256
COUNT, HALF = SLOTS, SLOTS + 1
LONG = (1 << 35, 1 << 26)
VMEM = pl.BlockSpec(memory_space=pltpu.VMEM)
SMEM = pl.BlockSpec(memory_space=pltpu.SMEM)
ANY = pl.BlockSpec(memory_space=pl.ANY)


def whole(
    kernel,
    ins,
    out_shape,
    name,
    cost,
    limit=4 << 20,
    specs=None,
    out_specs=None,
    scratch=(),
):
    return pl.pallas_call(
        kernel,
        in_specs=specs or [VMEM] * len(ins),
        out_specs=out_specs or jax.tree.map(lambda _: VMEM, out_shape),
        out_shape=out_shape,
        scratch_shapes=scratch,
        compiler_params=pltpu.CompilerParams(vmem_limit_bytes=limit),
        cost_estimate=pl.CostEstimate(
            flops=cost[0], bytes_accessed=cost[1], transcendentals=0
        ),
        name=name,
    )(*ins)


def copy_kernel(in_ref, out_ref):
    out_ref[...] = in_ref[...]


def side_by_side(table_ref, row, block_of):
    count = table_ref[COUNT, row]
    lhs = []
    for k in range(SLOTS):
        block = block_of(k)
        lhs.append(jnp.where(k < count, block, jnp.zeros_like(block)))
    return jnp.concatenate(lhs, axis=1)


def product(table_ref, row, lhs, stripe_ref):
    rhs = [stripe_ref[table_ref[k, row]] for k in range(SLOTS)]
    term = jnp.dot(
        lhs, jnp.concatenate(rhs, axis=0), preferred_element_type=jnp.float32
    )
    return term.astype(jnp.bfloat16)


def lhs_rows(table, blocks, far):
    step = 4

    def half(table_ref):
        return 1 - table_ref[HALF, 0] if far else table_ref[HALF, 0]

    def kernel(table_ref, blocks_ref, out_ref):
        base = pl.program_id(0) * step
        for i in range(step):
            row = 2 * (base + i) + half(table_ref)
            out_ref[i] = side_by_side(table_ref, row, lambda k: blocks_ref[i, 0, k])

    return pl.pallas_call(
        kernel,
        grid_spec=pltpu.PrefetchScalarGridSpec(
            num_scalar_prefetch=1,
            grid=(X * Y // step,),
            in_specs=[
                pl.BlockSpec(
                    (step, 1, SLOTS, BS, BS),
                    lambda i, table_ref: (i, half(table_ref), 0, 0, 0),
                )
            ],
            out_specs=pl.BlockSpec((step, BS, SLOTS * BS), lambda i, *_: (i, 0, 0)),
        ),
        out_shape=jax.ShapeDtypeStruct((X * Y, BS, SLOTS * BS), jnp.bfloat16),
        compiler_params=pltpu.CompilerParams(vmem_limit_bytes=6 << 20),
        cost_estimate=pl.CostEstimate(
            flops=0, bytes_accessed=4 << 20, transcendentals=0
        ),
        name="far_lhs" if far else "near_lhs",
    )(table, blocks)


def terms_kernel(
    table_ref,
    far_lhs_ref,
    near_lhs_ref,
    held_ref,
    across_ref,
    far_ref,
    near_ref,
    stripe_ref,
    made,
    sem,
):
    zh = table_ref[HALF, 0]
    for i, d in enumerate((0, 4, 2, 6, 1, 5, 3, 7)):
        stripe_ref[CORE * d] = held_ref[i]
        stripe_ref[CORE * d + 1] = across_ref[i]
    group = X * Y // sem.shape[0]
    stores = []
    for g in range(sem.shape[0]):
        for j in range(g * group, (g + 1) * group):
            made[j] = product(table_ref, 2 * j + zh, near_lhs_ref[j], stripe_ref)
        part = pl.ds(g * group, group)
        stores.append(
            pltpu.make_async_copy(made.at[part], near_ref.at[part], sem.at[g])
        )
        stores[-1].start()
    for j in range(X * Y):
        far_ref[j] = product(table_ref, 2 * j + 1 - zh, far_lhs_ref[j], stripe_ref)
    for store in stores:
        store.wait()


def total(parts):
    acc = parts[0].astype(jnp.float32)
    for part in parts[1:]:
        acc = acc + part.astype(jnp.float32)
    return acc


def send_kernel(parts_ref, out_ref):
    out_ref[...] = total([parts_ref[k] for k in range(X * Y)]).astype(jnp.bfloat16)


def finish_kernel(parts_ref, other_ref, weight_ref, bias_ref, out_ref):
    summed = total([parts_ref[k] for k in range(X * Y)]) + other_ref[...].astype(
        jnp.float32
    )
    hidden = jnp.dot(
        summed.astype(jnp.bfloat16),
        weight_ref[...],
        preferred_element_type=jnp.float32,
    )
    out_ref[...] = jnp.maximum(hidden + bias_ref[...], 0.0).astype(jnp.bfloat16)


def shard_table(block_col, row_count):
    zl, core, zh = (
        lax.axis_index(a).astype(jnp.int32) for a in ("zl", "core", "zh")
    )
    spots = block_col.T ^ (CORE * zl + core)
    counts = row_count.T
    return jnp.concatenate([spots, counts, jnp.full_like(counts, zh)], axis=0)


def local(features, blocks, block_col, row_count, weight, out_bias):
    bf16 = jnp.bfloat16
    table = shard_table(block_col, row_count)
    blocks = pltpu.with_memory_space_constraint(
        blocks.reshape(X * Y, ZH, SLOTS, BS, BS), pltpu.HBM
    )
    own = whole(
        copy_kernel,
        [features[None]],
        jax.ShapeDtypeStruct((1, BS, F), bf16),
        "own",
        LONG,
    )
    def hop(value, bit):
        return lax.ppermute(value, "zl", [(z, z ^ bit) for z in range(ZL)])

    def cross(value):
        return lax.ppermute(value, "core", [(0, 1), (1, 0)])

    p4, p2 = hop(features[None], 4), hop(own, 2)
    p4, table = lax.optimization_barrier((p4, table))
    p6 = hop(p4, 2)
    far_lhs = lhs_rows(table, blocks, True)
    p6, far_lhs = lax.optimization_barrier((p6, far_lhs))
    even = jnp.concatenate([own, p4, p2, p6], axis=0)
    even, table = lax.optimization_barrier((even, table))
    near_lhs = lhs_rows(table, blocks, False)
    odd, near_lhs = lax.optimization_barrier((hop(even, 1), near_lhs))
    held = jnp.concatenate([even, odd], axis=0)
    across = cross(held)
    half = (X * Y, BS, F)
    one = jax.ShapeDtypeStruct((BS, F), bf16)
    far_terms, near_terms = whole(
        terms_kernel,
        [table, far_lhs, near_lhs, held, across],
        [jax.ShapeDtypeStruct(half, bf16)] * 2,
        "terms",
        (4 * X * Y * SLOTS * BS * BS * F, 7 << 20),
        limit=8 << 20,
        specs=[SMEM] + [VMEM] * 4,
        out_specs=[VMEM, ANY],
        scratch=[
            pltpu.VMEM((CORE * ZL, BS, F), bf16),
            pltpu.VMEM(half, bf16),
            pltpu.SemaphoreType.DMA((2,)),
        ],
    )
    far_parts = lax.all_to_all(far_terms, ("x", "y"), 0, 0)
    near_parts = lax.all_to_all(near_terms, ("x", "y"), 0, 0)
    send = whole(send_kernel, [far_parts], one, "send", (0, 1 << 20))
    other = lax.ppermute(send, "zh", [(0, 1), (1, 0)])
    return whole(
        finish_kernel,
        [near_parts, other, weight, out_bias[None]],
        one,
        "finish",
        (2 * BS * F * F, 2 << 20),
    )


def solution(mesh):
    fine = Mesh(
        mesh.devices.reshape(ZL, CORE, X, Y, ZH), ("zl", "core", "x", "y", "zh")
    )
    row, col = ("zl", "core"), ("x", "y", "zh")
    return jax.shard_map(
        local,
        mesh=fine,
        in_specs=(
            P(row + col, None),
            P(row, col, None, None),
            P(row, col),
            P(row, col),
            P(),
            P(),
        ),
        out_specs=P(row + col, None),
        check_vma=False,
    )
```

```python
import jax
import jax.numpy as jnp
from jax import lax
from jax.experimental import pallas as pl
from jax.experimental.pallas import tpu as pltpu
from jax.sharding import Mesh, PartitionSpec as P

ZL, CORE, X, Y, ZH = 8, 2, 4, 4, 2
SLOTS, BS, F = 4, 128, 256
COUNT, HALF = SLOTS, SLOTS + 1
LONG = (1 << 35, 1 << 26)
VMEM = pl.BlockSpec(memory_space=pltpu.VMEM)
SMEM = pl.BlockSpec(memory_space=pltpu.SMEM)
ANY = pl.BlockSpec(memory_space=pl.ANY)


def whole(
    kernel,
    ins,
    out_shape,
    name,
    cost,
    limit=4 << 20,
    specs=None,
    out_specs=None,
    scratch=(),
):
    return pl.pallas_call(
        kernel,
        in_specs=specs or [VMEM] * len(ins),
        out_specs=out_specs or jax.tree.map(lambda _: VMEM, out_shape),
        out_shape=out_shape,
        scratch_shapes=scratch,
        compiler_params=pltpu.CompilerParams(vmem_limit_bytes=limit),
        cost_estimate=pl.CostEstimate(
            flops=cost[0], bytes_accessed=cost[1], transcendentals=0
        ),
        name=name,
    )(*ins)


def copy_kernel(in_ref, out_ref):
    out_ref[...] = in_ref[...]


def side_by_side(table_ref, row, block_of):
    count = table_ref[COUNT, row]
    lhs = []
    for k in range(SLOTS):
        block = block_of(k)
        lhs.append(jnp.where(k < count, block, jnp.zeros_like(block)))
    return jnp.concatenate(lhs, axis=1)


def product(table_ref, row, lhs, stripe_ref):
    rhs = [stripe_ref[table_ref[k, row]] for k in range(SLOTS)]
    term = jnp.dot(
        lhs, jnp.concatenate(rhs, axis=0), preferred_element_type=jnp.float32
    )
    return term.astype(jnp.bfloat16)


def far_lhs_kernel(table_ref, blocks_ref, out_ref):
    step = blocks_ref.shape[0]
    base = pl.program_id(0) * step
    for i in range(step):
        row = 2 * (base + i) + 1 - table_ref[HALF, 0]
        out_ref[i] = side_by_side(table_ref, row, lambda k: blocks_ref[i, 0, k])


def far_lhs_rows(table, blocks):
    step = 4
    return pl.pallas_call(
        far_lhs_kernel,
        grid_spec=pltpu.PrefetchScalarGridSpec(
            num_scalar_prefetch=1,
            grid=(X * Y // step,),
            in_specs=[
                pl.BlockSpec(
                    (step, 1, SLOTS, BS, BS),
                    lambda i, table_ref: (i, 1 - table_ref[HALF, 0], 0, 0, 0),
                )
            ],
            out_specs=pl.BlockSpec((step, BS, SLOTS * BS), lambda i, *_: (i, 0, 0)),
        ),
        out_shape=jax.ShapeDtypeStruct((X * Y, BS, SLOTS * BS), jnp.bfloat16),
        compiler_params=pltpu.CompilerParams(vmem_limit_bytes=6 << 20),
        cost_estimate=pl.CostEstimate(
            flops=0, bytes_accessed=4 << 20, transcendentals=0
        ),
        name="far_lhs",
    )(table, blocks)


def far_kernel(table_ref, lhs_ref, *refs):
    held, across, stripe_ref, out_ref, made, sem = refs
    for i, d in enumerate((0, 1, 4, 2, 6, 5, 3, 7)):
        stripe_ref[CORE * d] = held[i]
        stripe_ref[CORE * d + 1] = across[i]
    group = X * Y // sem.shape[0]
    stores = []
    for g in range(sem.shape[0]):
        for j in range(g * group, (g + 1) * group):
            made[j] = product(
                table_ref, 2 * j + 1 - table_ref[HALF, 0], lhs_ref[j], stripe_ref
            )
        part = pl.ds(g * group, group)
        stores.append(
            pltpu.make_async_copy(made.at[part], out_ref.at[part], sem.at[g])
        )
        stores[-1].start()
    for store in stores:
        store.wait()


def near_kernel(table_ref, blocks_ref, stripe_ref, out_ref):
    step = blocks_ref.shape[0]
    base = pl.program_id(0) * step
    for i in range(step):
        row = 2 * (base + i) + table_ref[HALF, 0]
        lhs = side_by_side(table_ref, row, lambda k: blocks_ref[i, 0, k])
        out_ref[i] = product(table_ref, row, lhs, stripe_ref)


def near_half(table, blocks, stripe):
    step = 4
    return pl.pallas_call(
        near_kernel,
        grid_spec=pltpu.PrefetchScalarGridSpec(
            num_scalar_prefetch=1,
            grid=(X * Y // step,),
            in_specs=[
                pl.BlockSpec(
                    (step, 1, SLOTS, BS, BS),
                    lambda i, table_ref: (i, table_ref[HALF, 0], 0, 0, 0),
                ),
                VMEM,
            ],
            out_specs=pl.BlockSpec((step, BS, F), lambda i, *_: (i, 0, 0)),
        ),
        out_shape=jax.ShapeDtypeStruct((X * Y, BS, F), jnp.bfloat16),
        compiler_params=pltpu.CompilerParams(vmem_limit_bytes=8 << 20),
        cost_estimate=pl.CostEstimate(
            flops=2 * X * Y * SLOTS * BS * BS * F,
            bytes_accessed=4 << 20,
            transcendentals=0,
        ),
        name="near_terms",
    )(table, blocks, stripe)


def total(parts):
    acc = parts[0].astype(jnp.float32)
    for part in parts[1:]:
        acc = acc + part.astype(jnp.float32)
    return acc


def send_kernel(parts_ref, out_ref):
    out_ref[...] = total([parts_ref[k] for k in range(X * Y)]).astype(jnp.bfloat16)


def finish_kernel(parts_ref, other_ref, weight_ref, bias_ref, out_ref):
    summed = total([parts_ref[k] for k in range(X * Y)]) + other_ref[...].astype(
        jnp.float32
    )
    hidden = jnp.dot(
        summed.astype(jnp.bfloat16),
        weight_ref[...],
        preferred_element_type=jnp.float32,
    )
    out_ref[...] = jnp.maximum(hidden + bias_ref[...], 0.0).astype(jnp.bfloat16)


def shard_table(block_col, row_count):
    zl, core, zh = (
        lax.axis_index(a).astype(jnp.int32) for a in ("zl", "core", "zh")
    )
    spots = block_col.T ^ (CORE * zl + core)
    counts = row_count.T
    return jnp.concatenate([spots, counts, jnp.full_like(counts, zh)], axis=0)


def local(features, blocks, block_col, row_count, weight, out_bias):
    bf16 = jnp.bfloat16
    table = shard_table(block_col, row_count)
    blocks = pltpu.with_memory_space_constraint(
        blocks.reshape(X * Y, ZH, SLOTS, BS, BS), pltpu.HBM
    )
    own = whole(
        copy_kernel,
        [features[None]],
        jax.ShapeDtypeStruct((1, BS, F), bf16),
        "own",
        LONG,
    )
    def hop(value, bit):
        return lax.ppermute(value, "zl", [(z, z ^ bit) for z in range(ZL)])

    def cross(value):
        return lax.ppermute(value, "core", [(0, 1), (1, 0)])

    p4, p2 = hop(features[None], 4), hop(own, 2)
    p4, table, mine = lax.optimization_barrier((p4, table, own))
    p6, p1 = hop(p4, 2), hop(mine, 1)
    three = jnp.concatenate([p4, p2, p6], axis=0)
    three, table = lax.optimization_barrier((three, table))
    far_lhs = far_lhs_rows(table, blocks)
    odd, far_lhs = lax.optimization_barrier((hop(three, 1), far_lhs))
    held = jnp.concatenate([own, p1, p4, p2, p6, odd], axis=0)
    across = cross(held)
    half = (X * Y, BS, F)
    one = jax.ShapeDtypeStruct((BS, F), bf16)
    stripe, far_terms = whole(
        far_kernel,
        [table, far_lhs, held, across],
        [jax.ShapeDtypeStruct(half, bf16)] * 2,
        "far_terms",
        (2 * X * Y * SLOTS * BS * BS * F, 4 << 20),
        limit=8 << 20,
        specs=[SMEM, VMEM, VMEM, VMEM],
        out_specs=[VMEM, ANY],
        scratch=[pltpu.VMEM(half, bf16), pltpu.SemaphoreType.DMA((4,))],
    )
    near_terms = near_half(table, blocks, stripe)
    far_parts = lax.all_to_all(far_terms, ("x", "y"), 0, 0)
    near_parts = lax.all_to_all(near_terms, ("x", "y"), 0, 0)
    send = whole(send_kernel, [far_parts], one, "send", (0, 1 << 20))
    other = lax.ppermute(send, "zh", [(0, 1), (1, 0)])
    return whole(
        finish_kernel,
        [near_parts, other, weight, out_bias[None]],
        one,
        "finish",
        (2 * BS * F * F, 2 << 20),
    )


def solution(mesh):
    fine = Mesh(
        mesh.devices.reshape(ZL, CORE, X, Y, ZH), ("zl", "core", "x", "y", "zh")
    )
    row, col = ("zl", "core"), ("x", "y", "zh")
    return jax.shard_map(
        local,
        mesh=fine,
        in_specs=(
            P(row + col, None),
            P(row, col, None, None),
            P(row, col),
            P(row, col),
            P(),
            P(),
        ),
        out_specs=P(row + col, None),
        check_vma=False,
    )
```

```python
import jax
import jax.numpy as jnp
from jax import lax
from jax.experimental import pallas as pl
from jax.experimental.pallas import tpu as pltpu
from jax.sharding import Mesh, PartitionSpec as P

ZL, CORE, X, Y, ZH = 8, 2, 4, 4, 2
SLOTS, BS, F = 4, 128, 256
COUNT, HALF = SLOTS, SLOTS + 1
LONG = (1 << 35, 1 << 26)
VMEM = pl.BlockSpec(memory_space=pltpu.VMEM)
SMEM = pl.BlockSpec(memory_space=pltpu.SMEM)
ANY = pl.BlockSpec(memory_space=pl.ANY)


def whole(
    kernel,
    ins,
    out_shape,
    name,
    cost,
    limit=4 << 20,
    specs=None,
    out_specs=None,
    scratch=(),
):
    return pl.pallas_call(
        kernel,
        in_specs=specs or [VMEM] * len(ins),
        out_specs=out_specs or jax.tree.map(lambda _: VMEM, out_shape),
        out_shape=out_shape,
        scratch_shapes=scratch,
        compiler_params=pltpu.CompilerParams(vmem_limit_bytes=limit),
        cost_estimate=pl.CostEstimate(
            flops=cost[0], bytes_accessed=cost[1], transcendentals=0
        ),
        name=name,
    )(*ins)


def copy_kernel(in_ref, out_ref):
    out_ref[...] = in_ref[...]


def side_by_side(table_ref, row, block_of):
    count = table_ref[COUNT, row]
    lhs = []
    for k in range(SLOTS):
        block = block_of(k)
        lhs.append(jnp.where(k < count, block, jnp.zeros_like(block)))
    return jnp.concatenate(lhs, axis=1)


def product(table_ref, row, lhs, stripe_ref):
    rhs = [stripe_ref[table_ref[k, row]] for k in range(SLOTS)]
    term = jnp.dot(
        lhs, jnp.concatenate(rhs, axis=0), preferred_element_type=jnp.float32
    )
    return term.astype(jnp.bfloat16)


def far_lhs_kernel(table_ref, blocks_ref, out_ref):
    step = blocks_ref.shape[0]
    base = pl.program_id(0) * step
    for i in range(step):
        row = 2 * (base + i) + 1 - table_ref[HALF, 0]
        out_ref[i] = side_by_side(table_ref, row, lambda k: blocks_ref[i, 0, k])


def far_lhs_rows(table, blocks):
    step = 4
    return pl.pallas_call(
        far_lhs_kernel,
        grid_spec=pltpu.PrefetchScalarGridSpec(
            num_scalar_prefetch=1,
            grid=(X * Y // step,),
            in_specs=[
                pl.BlockSpec(
                    (step, 1, SLOTS, BS, BS),
                    lambda i, table_ref: (i, 1 - table_ref[HALF, 0], 0, 0, 0),
                )
            ],
            out_specs=pl.BlockSpec((step, BS, SLOTS * BS), lambda i, *_: (i, 0, 0)),
        ),
        out_shape=jax.ShapeDtypeStruct((X * Y, BS, SLOTS * BS), jnp.bfloat16),
        compiler_params=pltpu.CompilerParams(vmem_limit_bytes=6 << 20),
        cost_estimate=pl.CostEstimate(
            flops=0, bytes_accessed=4 << 20, transcendentals=0
        ),
        name="far_lhs",
    )(table, blocks)


def far_kernel(table_ref, lhs_ref, *refs):
    held, across, stripe_ref, out_ref, made, sem = refs
    for i, d in enumerate((0, 1, 4, 2, 6, 3, 5, 7)):
        stripe_ref[CORE * d] = held[i]
        stripe_ref[CORE * d + 1] = across[i]
    group = X * Y // sem.shape[0]
    stores = []
    for g in range(sem.shape[0]):
        for j in range(g * group, (g + 1) * group):
            made[j] = product(
                table_ref, 2 * j + 1 - table_ref[HALF, 0], lhs_ref[j], stripe_ref
            )
        part = pl.ds(g * group, group)
        stores.append(
            pltpu.make_async_copy(made.at[part], out_ref.at[part], sem.at[g])
        )
        stores[-1].start()
    for store in stores:
        store.wait()


def near_kernel(table_ref, blocks_ref, stripe_ref, out_ref):
    step = blocks_ref.shape[0]
    base = pl.program_id(0) * step
    for i in range(step):
        row = 2 * (base + i) + table_ref[HALF, 0]
        lhs = side_by_side(table_ref, row, lambda k: blocks_ref[i, 0, k])
        out_ref[i] = product(table_ref, row, lhs, stripe_ref)


def near_half(table, blocks, stripe):
    step = 4
    return pl.pallas_call(
        near_kernel,
        grid_spec=pltpu.PrefetchScalarGridSpec(
            num_scalar_prefetch=1,
            grid=(X * Y // step,),
            in_specs=[
                pl.BlockSpec(
                    (step, 1, SLOTS, BS, BS),
                    lambda i, table_ref: (i, table_ref[HALF, 0], 0, 0, 0),
                ),
                VMEM,
            ],
            out_specs=pl.BlockSpec((step, BS, F), lambda i, *_: (i, 0, 0)),
        ),
        out_shape=jax.ShapeDtypeStruct((X * Y, BS, F), jnp.bfloat16),
        compiler_params=pltpu.CompilerParams(vmem_limit_bytes=8 << 20),
        cost_estimate=pl.CostEstimate(
            flops=2 * X * Y * SLOTS * BS * BS * F,
            bytes_accessed=4 << 20,
            transcendentals=0,
        ),
        name="near_terms",
    )(table, blocks, stripe)


def total(parts):
    acc = parts[0].astype(jnp.float32)
    for part in parts[1:]:
        acc = acc + part.astype(jnp.float32)
    return acc


def send_kernel(parts_ref, out_ref):
    out_ref[...] = total([parts_ref[k] for k in range(X * Y)]).astype(jnp.bfloat16)


def finish_kernel(parts_ref, other_ref, weight_ref, bias_ref, out_ref):
    summed = total([parts_ref[k] for k in range(X * Y)]) + other_ref[...].astype(
        jnp.float32
    )
    hidden = jnp.dot(
        summed.astype(jnp.bfloat16),
        weight_ref[...],
        preferred_element_type=jnp.float32,
    )
    out_ref[...] = jnp.maximum(hidden + bias_ref[...], 0.0).astype(jnp.bfloat16)


def shard_table(block_col, row_count):
    zl, core, zh = (
        lax.axis_index(a).astype(jnp.int32) for a in ("zl", "core", "zh")
    )
    spots = block_col.T ^ (CORE * zl + core)
    counts = row_count.T
    return jnp.concatenate([spots, counts, jnp.full_like(counts, zh)], axis=0)


def local(features, blocks, block_col, row_count, weight, out_bias):
    bf16 = jnp.bfloat16
    table = shard_table(block_col, row_count)
    blocks = pltpu.with_memory_space_constraint(
        blocks.reshape(X * Y, ZH, SLOTS, BS, BS), pltpu.HBM
    )
    own = whole(
        copy_kernel,
        [features[None]],
        jax.ShapeDtypeStruct((1, BS, F), bf16),
        "own",
        LONG,
    )
    def hop(value, bit):
        return lax.ppermute(value, "zl", [(z, z ^ bit) for z in range(ZL)])

    def cross(value):
        return lax.ppermute(value, "core", [(0, 1), (1, 0)])

    p4, p2 = hop(features[None], 4), hop(own, 2)
    p4, table, mine = lax.optimization_barrier((p4, table, own))
    p6, p1, p3 = hop(p4, 2), hop(mine, 1), hop(p2, 1)
    two = jnp.concatenate([p4, p6], axis=0)
    two, table = lax.optimization_barrier((two, table))
    far_lhs = far_lhs_rows(table, blocks)
    odd, far_lhs = lax.optimization_barrier((hop(two, 1), far_lhs))
    held = jnp.concatenate([own, p1, p4, p2, p6, p3, odd], axis=0)
    across = cross(held)
    half = (X * Y, BS, F)
    one = jax.ShapeDtypeStruct((BS, F), bf16)
    stripe, far_terms = whole(
        far_kernel,
        [table, far_lhs, held, across],
        [jax.ShapeDtypeStruct(half, bf16)] * 2,
        "far_terms",
        (2 * X * Y * SLOTS * BS * BS * F, 4 << 20),
        limit=8 << 20,
        specs=[SMEM, VMEM, VMEM, VMEM],
        out_specs=[VMEM, ANY],
        scratch=[pltpu.VMEM(half, bf16), pltpu.SemaphoreType.DMA((4,))],
    )
    near_terms = near_half(table, blocks, stripe)
    far_parts = lax.all_to_all(far_terms, ("x", "y"), 0, 0)
    near_parts = lax.all_to_all(near_terms, ("x", "y"), 0, 0)
    send = whole(send_kernel, [far_parts], one, "send", (0, 1 << 20))
    other = lax.ppermute(send, "zh", [(0, 1), (1, 0)])
    return whole(
        finish_kernel,
        [near_parts, other, weight, out_bias[None]],
        one,
        "finish",
        (2 * BS * F * F, 2 << 20),
    )


def solution(mesh):
    fine = Mesh(
        mesh.devices.reshape(ZL, CORE, X, Y, ZH), ("zl", "core", "x", "y", "zh")
    )
    row, col = ("zl", "core"), ("x", "y", "zh")
    return jax.shard_map(
        local,
        mesh=fine,
        in_specs=(
            P(row + col, None),
            P(row, col, None, None),
            P(row, col),
            P(row, col),
            P(),
            P(),
        ),
        out_specs=P(row + col, None),
        check_vma=False,
    )
```

```python
import jax
import jax.numpy as jnp
from jax import lax
from jax.experimental import pallas as pl
from jax.experimental.pallas import tpu as pltpu
from jax.sharding import Mesh, PartitionSpec as P

ZL, CORE, X, Y, ZH = 8, 2, 4, 4, 2
SLOTS, BS, F = 4, 128, 256
COUNT, HALF = SLOTS, SLOTS + 1
LONG = (1 << 35, 1 << 26)
VMEM = pl.BlockSpec(memory_space=pltpu.VMEM)
SMEM = pl.BlockSpec(memory_space=pltpu.SMEM)
ANY = pl.BlockSpec(memory_space=pl.ANY)


def whole(
    kernel,
    ins,
    out_shape,
    name,
    cost,
    limit=4 << 20,
    specs=None,
    out_specs=None,
    scratch=(),
):
    return pl.pallas_call(
        kernel,
        in_specs=specs or [VMEM] * len(ins),
        out_specs=out_specs or jax.tree.map(lambda _: VMEM, out_shape),
        out_shape=out_shape,
        scratch_shapes=scratch,
        compiler_params=pltpu.CompilerParams(vmem_limit_bytes=limit),
        cost_estimate=pl.CostEstimate(
            flops=cost[0], bytes_accessed=cost[1], transcendentals=0
        ),
        name=name,
    )(*ins)


def copy_kernel(in_ref, out_ref):
    out_ref[...] = in_ref[...]


def side_by_side(table_ref, row, block_of):
    count = table_ref[COUNT, row]
    lhs = []
    for k in range(SLOTS):
        block = block_of(k)
        lhs.append(jnp.where(k < count, block, jnp.zeros_like(block)))
    return jnp.concatenate(lhs, axis=1)


def product(table_ref, row, lhs, stripe_ref):
    rhs = [stripe_ref[table_ref[k, row]] for k in range(SLOTS)]
    term = jnp.dot(
        lhs, jnp.concatenate(rhs, axis=0), preferred_element_type=jnp.float32
    )
    return term.astype(jnp.bfloat16)


def far_lhs_kernel(table_ref, blocks_ref, out_ref):
    step = blocks_ref.shape[0]
    base = pl.program_id(0) * step
    for i in range(step):
        row = 2 * (base + i) + 1 - table_ref[HALF, 0]
        out_ref[i] = side_by_side(table_ref, row, lambda k: blocks_ref[i, 0, k])


def far_lhs_rows(table, blocks):
    step = 4
    return pl.pallas_call(
        far_lhs_kernel,
        grid_spec=pltpu.PrefetchScalarGridSpec(
            num_scalar_prefetch=1,
            grid=(X * Y // step,),
            in_specs=[
                pl.BlockSpec(
                    (step, 1, SLOTS, BS, BS),
                    lambda i, table_ref: (i, 1 - table_ref[HALF, 0], 0, 0, 0),
                )
            ],
            out_specs=pl.BlockSpec((step, BS, SLOTS * BS), lambda i, *_: (i, 0, 0)),
        ),
        out_shape=jax.ShapeDtypeStruct((X * Y, BS, SLOTS * BS), jnp.bfloat16),
        compiler_params=pltpu.CompilerParams(vmem_limit_bytes=6 << 20),
        cost_estimate=pl.CostEstimate(
            flops=0, bytes_accessed=4 << 20, transcendentals=0
        ),
        name="far_lhs",
    )(table, blocks)


def far_kernel(table_ref, lhs_ref, *refs):
    held, across, stripe_ref, out_ref, made, sem = refs
    for i, d in enumerate((0, 1, 4, 2, 6, 5, 3, 7)):
        stripe_ref[CORE * d] = held[i]
        stripe_ref[CORE * d + 1] = across[i]
    group = X * Y // sem.shape[0]
    stores = []
    for g in range(sem.shape[0]):
        for j in range(g * group, (g + 1) * group):
            made[j] = product(
                table_ref, 2 * j + 1 - table_ref[HALF, 0], lhs_ref[j], stripe_ref
            )
        part = pl.ds(g * group, group)
        stores.append(
            pltpu.make_async_copy(made.at[part], out_ref.at[part], sem.at[g])
        )
        stores[-1].start()
    for store in stores:
        store.wait()


def near_kernel(table_ref, blocks_ref, stripe_ref, out_ref):
    step = blocks_ref.shape[0]
    base = pl.program_id(0) * step
    for i in range(step):
        row = 2 * (base + i) + table_ref[HALF, 0]
        lhs = side_by_side(table_ref, row, lambda k: blocks_ref[i, 0, k])
        out_ref[i] = product(table_ref, row, lhs, stripe_ref)


def near_half(table, blocks, stripe):
    step = 4
    return pl.pallas_call(
        near_kernel,
        grid_spec=pltpu.PrefetchScalarGridSpec(
            num_scalar_prefetch=1,
            grid=(X * Y // step,),
            in_specs=[
                pl.BlockSpec(
                    (step, 1, SLOTS, BS, BS),
                    lambda i, table_ref: (i, table_ref[HALF, 0], 0, 0, 0),
                ),
                VMEM,
            ],
            out_specs=pl.BlockSpec((step, BS, F), lambda i, *_: (i, 0, 0)),
        ),
        out_shape=jax.ShapeDtypeStruct((X * Y, BS, F), jnp.bfloat16),
        compiler_params=pltpu.CompilerParams(vmem_limit_bytes=8 << 20),
        cost_estimate=pl.CostEstimate(
            flops=2 * X * Y * SLOTS * BS * BS * F,
            bytes_accessed=4 << 20,
            transcendentals=0,
        ),
        name="near_terms",
    )(table, blocks, stripe)


def total(parts):
    acc = parts[0].astype(jnp.float32)
    for part in parts[1:]:
        acc = acc + part.astype(jnp.float32)
    return acc


def send_kernel(parts_ref, out_ref):
    out_ref[...] = total([parts_ref[k] for k in range(X * Y)]).astype(jnp.bfloat16)


def near_hidden_kernel(parts_ref, weight_ref, bias_ref, out_ref):
    summed = total([parts_ref[k] for k in range(X * Y)]).astype(jnp.bfloat16)
    out_ref[...] = (
        jnp.dot(summed, weight_ref[...], preferred_element_type=jnp.float32)
        + bias_ref[...]
    )


def finish_kernel(other_ref, hidden_ref, weight_ref, out_ref):
    hidden = hidden_ref[...] + jnp.dot(
        other_ref[...], weight_ref[...], preferred_element_type=jnp.float32
    )
    out_ref[...] = jnp.maximum(hidden, 0.0).astype(jnp.bfloat16)


def shard_table(block_col, row_count):
    zl, core, zh = (
        lax.axis_index(a).astype(jnp.int32) for a in ("zl", "core", "zh")
    )
    spots = block_col.T ^ (CORE * zl + core)
    counts = row_count.T
    return jnp.concatenate([spots, counts, jnp.full_like(counts, zh)], axis=0)


def local(features, blocks, block_col, row_count, weight, out_bias):
    bf16 = jnp.bfloat16
    table = shard_table(block_col, row_count)
    blocks = pltpu.with_memory_space_constraint(
        blocks.reshape(X * Y, ZH, SLOTS, BS, BS), pltpu.HBM
    )
    own = whole(
        copy_kernel,
        [features[None]],
        jax.ShapeDtypeStruct((1, BS, F), bf16),
        "own",
        LONG,
    )
    def hop(value, bit):
        return lax.ppermute(value, "zl", [(z, z ^ bit) for z in range(ZL)])

    def cross(value):
        return lax.ppermute(value, "core", [(0, 1), (1, 0)])

    p4, p2 = hop(features[None], 4), hop(own, 2)
    p4, table, mine = lax.optimization_barrier((p4, table, own))
    p6, p1 = hop(p4, 2), hop(mine, 1)
    three = jnp.concatenate([p4, p2, p6], axis=0)
    three, table = lax.optimization_barrier((three, table))
    far_lhs = far_lhs_rows(table, blocks)
    odd, far_lhs = lax.optimization_barrier((hop(three, 1), far_lhs))
    held = jnp.concatenate([own, p1, p4, p2, p6, odd], axis=0)
    across = cross(held)
    half = (X * Y, BS, F)
    one = jax.ShapeDtypeStruct((BS, F), bf16)
    stripe, far_terms = whole(
        far_kernel,
        [table, far_lhs, held, across],
        [jax.ShapeDtypeStruct(half, bf16)] * 2,
        "far_terms",
        (2 * X * Y * SLOTS * BS * BS * F, 4 << 20),
        limit=8 << 20,
        specs=[SMEM, VMEM, VMEM, VMEM],
        out_specs=[VMEM, ANY],
        scratch=[pltpu.VMEM(half, bf16), pltpu.SemaphoreType.DMA((4,))],
    )
    near_terms = near_half(table, blocks, stripe)
    far_parts = lax.all_to_all(far_terms, ("x", "y"), 0, 0)
    near_parts = lax.all_to_all(near_terms, ("x", "y"), 0, 0)
    send = whole(send_kernel, [far_parts], one, "send", (0, 1 << 20))
    other = lax.ppermute(send, "zh", [(0, 1), (1, 0)])
    hidden = whole(
        near_hidden_kernel,
        [near_parts, weight, out_bias[None]],
        jax.ShapeDtypeStruct((BS, F), jnp.float32),
        "near_hidden",
        (2 * BS * F * F, 2 << 20),
    )
    return whole(
        finish_kernel, [other, hidden, weight], one, "finish", (2 * BS * F * F, 1 << 19)
    )


def solution(mesh):
    fine = Mesh(
        mesh.devices.reshape(ZL, CORE, X, Y, ZH), ("zl", "core", "x", "y", "zh")
    )
    row, col = ("zl", "core"), ("x", "y", "zh")
    return jax.shard_map(
        local,
        mesh=fine,
        in_specs=(
            P(row + col, None),
            P(row, col, None, None),
            P(row, col),
            P(row, col),
            P(),
            P(),
        ),
        out_specs=P(row + col, None),
        check_vma=False,
    )
```
